256 devices in a mesh: ctx: 64 (over x, z, core), tp: 4 (over y).
Axes of the slice: x: 4, y: 4, z: 8, core: 2. Of those that a mesh axis runs over, the one named last changes fastest.
Arguments:
- out_gate: bfloat16 [8192, 8192], P('ctx', 'tp'), may hold values from -128 to 128
- key_proj: bfloat16 [8192, 8192], P('ctx', 'tp'), may hold values from -6 to 6
- value_proj: bfloat16 [8192, 8192], P('ctx', 'tp'), may hold values from -6 to 6
- residue: float32 [512, 16], P('tp'), may hold values from -1 to 1
- log_decay: float32 [512, 16], P('tp'), may hold values from -13 to -3
- skip: float32 [8192], P('tp'), may hold values from -4 to 4
- gain: float32 [8192], P('tp'), may hold values from 0.1 to 1.9
- cotangent: bfloat16 [8192, 8192], P('ctx', 'tp'), may hold values from -6 to 6
Outputs:
- mixer_out: bfloat16 [8192, 8192], P('ctx', 'tp')
- grad_q: bfloat16 [8192, 8192], P('ctx', 'tp')
- grad_k: bfloat16 [8192, 8192], P('ctx', 'tp')
- grad_v: bfloat16 [8192, 8192], P('ctx', 'tp')
- grad_residue: float32 [512, 16], P('tp')
- grad_log_decay: float32 [512, 16], P('tp')
The draws below stay inside these ranges and needn't reach their ends.
All inputs are finite; a program needn't handle non-finite values.
Results may differ from the reference program's by a relative error of at most 0.0013.
Values sent between devices are 32-bit elements; how exact they have to be, the bound alone decides.
No kernel may reach another device: no remote copies, remote signals or barrier semaphores. Data moves between devices by JAX's collectives and lax.ppermute only.
A program may use at most 128 MiB of HBM per device.

```python
import math
import jax
import jax.numpy as jnp
from jax import lax

D = 8192
GROUP = 16
ORDER = 16
TOKENS = 8192


def mode_rates(key):
    pick_key, slow_key, fast_key = jax.random.split(jax.random.fold_in(key, 17), 3)
    shape = (D // GROUP, ORDER)
    slow = jnp.exp(jax.random.uniform(slow_key, shape, minval=math.log(0.3 / TOKENS), maxval=math.log(2.0 / TOKENS)))
    fast = jnp.exp(jax.random.uniform(fast_key, shape, minval=math.log(1.0 / 50.0), maxval=math.log(1.0 / 30.0)))
    share = 0.5
    chosen = jax.random.uniform(pick_key, shape) < share
    return jnp.where(chosen, slow, fast)


def draw_log_decay(key, part):
    return jnp.log(mode_rates(key)).astype(jnp.float32)


def draw_residue(key, part):
    rates = mode_rates(key)
    values = jax.random.truncated_normal(jax.random.fold_in(key, 29), -3.0, 3.0, rates.shape)
    return (values * jnp.sqrt(2.0 * rates)).astype(jnp.float32)


def draw_out_gate(key, part):
    base_key, row_key, col_key = jax.random.split(jax.random.fold_in(key, 3), 3)
    base = jax.random.truncated_normal(base_key, -4.0, 4.0, (TOKENS, D))
    rising = 0.5
    row_scale = 10.0 ** jax.random.uniform(row_key, (TOKENS, 1))
    channel_pos = jnp.arange(D, dtype=jnp.float32)[None, :] / D
    col_scale = 10.0 ** (rising * channel_pos + (1.0 - rising) * jax.random.uniform(col_key, (1, D)))
    return (0.3 * base * row_scale * col_scale).astype(jnp.bfloat16)


def block_scale(rng, shape, cuts, least, largest):
    level = 1.0
    for dim, parts in cuts:
        heights = jax.random.uniform(jax.random.fold_in(jax.random.fold_in(rng, 6), dim), (parts,), jnp.float32, least / len(cuts), largest / len(cuts))
        level = level * jnp.repeat(jnp.exp(heights), shape[dim] // parts).reshape((-1,) + (1,) * (len(shape) - 1 - dim))
    return level


def noise(own_key, dims, deviation, reach, cuts=(), held_as=jnp.bfloat16):
    factor_of = block_scale(own_key, dims, cuts, -0.22, 0.18) if cuts else 1.0
    values = jax.random.normal(own_key, dims, jnp.float32) * deviation * factor_of
    return jnp.minimum(jnp.maximum(values, -reach), reach).astype(held_as)


def setup_inputs(seed: int = 0) -> dict:
    keys = jax.random.split(jax.random.key(seed), 9)
    return {
        "out_gate": draw_out_gate(jax.random.fold_in(keys[8], 71), 0),
        "key_proj": noise(keys[1], (TOKENS, D), 1.0, 6.0, ((0, 64), (1, 4))),
        "value_proj": noise(keys[2], (TOKENS, D), 1.0, 6.0, ((0, 64), (1, 4))),
        "residue": draw_residue(jax.random.fold_in(keys[8], 71), 0),
        "log_decay": draw_log_decay(jax.random.fold_in(keys[8], 71), 0),
        "skip": noise(keys[5], (D,), 1.0, 4.0, ((0, 4),), jnp.float32),
        "gain": jnp.clip(1.0 + 0.18 * jax.random.normal(keys[6], (D,), jnp.float32), 0.1, 1.9),
        "cotangent": noise(keys[7], (TOKENS, D), 1.0, 6.0, ((0, 64), (1, 4))),
    }


EPSILON = 1e-06

def causal_conv(filter_taps, signal):
    seq_len = signal.shape[-1]
    padded_len = 2 * seq_len
    spectrum = jnp.fft.rfft(filter_taps, padded_len) * jnp.fft.rfft(signal, padded_len, axis=-1)
    return jnp.fft.irfft(spectrum, padded_len, axis=-1)[..., :seq_len]

def reference(out_gate, key_proj, value_proj, residue, log_decay, skip, gain, cotangent):
    seq_len, channel_count = out_gate.shape
    groups = residue.shape[0]
    gate_full = out_gate.astype(jnp.float32)
    key_full = key_proj.astype(jnp.float32)
    value_full = value_proj.astype(jnp.float32)
    signal = key_full * value_full
    decay_rate = jnp.exp(log_decay)
    lag_index = jnp.arange(seq_len, dtype=jnp.float32)

    def group_taps(residue_row, rate_row):
        return lax.optimization_barrier(jnp.sum(residue_row[:, None] * jnp.exp(-rate_row[:, None] * lag_index[None, :]), axis=0))
    signal_groups = signal.T.reshape(groups, GROUP, seq_len)

    def forward_group(inputs):
        residue_row, rate_row, group_signal = inputs
        return causal_conv(group_taps(residue_row, rate_row), group_signal)
    convolved = lax.map(forward_group, (residue, decay_rate, signal_groups)).reshape(channel_count, seq_len).T
    mixed = convolved + skip * signal
    premix = gate_full * mixed
    inverse = lax.rsqrt(lax.optimization_barrier(jnp.mean(premix * premix, axis=1, keepdims=True)) + EPSILON)
    normed = premix * inverse
    mixer_out = (normed * gain).astype(jnp.bfloat16)
    pull = cotangent.astype(jnp.float32) * gain
    dpre = (pull - normed * lax.optimization_barrier(jnp.mean(pull * normed, axis=1, keepdims=True))) * inverse
    grad_q = (dpre * mixed).astype(jnp.bfloat16)
    weight = dpre * gate_full
    grouped_weight_table = weight.T.reshape(groups, GROUP, seq_len)

    def backward_group(inputs):
        residue_row, rate_row, group_weight, group_signal = inputs
        filter_taps = group_taps(residue_row, rate_row)
        backward_part = jnp.flip(causal_conv(filter_taps, jnp.flip(group_weight, -1)), -1)
        padded_len = 2 * seq_len
        cross = jnp.fft.rfft(group_weight, padded_len, axis=-1) * jnp.conj(jnp.fft.rfft(group_signal, padded_len, axis=-1))
        lagged = lax.optimization_barrier(jnp.sum(jnp.fft.irfft(cross, padded_len, axis=-1)[:, :seq_len], axis=0))
        decay_table = jnp.exp(-rate_row[:, None] * lag_index[None, :])
        residue_grad = lax.optimization_barrier(jnp.sum(decay_table * lagged[None, :], axis=1))
        moment_grad = lax.optimization_barrier(jnp.sum(decay_table * lag_index[None, :] * lagged[None, :], axis=1))
        return (backward_part, residue_grad, -residue_row * rate_row * moment_grad)
    backward_part, residue_grad, decay_grad = lax.map(backward_group, (residue, decay_rate, grouped_weight_table, signal_groups))
    grad_signal = backward_part.reshape(channel_count, seq_len).T + skip * weight
    grad_k = (grad_signal * value_full).astype(jnp.bfloat16)
    grad_v = (grad_signal * key_full).astype(jnp.bfloat16)
    return (mixer_out, grad_q, grad_k, grad_v, residue_grad / seq_len, decay_grad / seq_len)
```

```python
import functools

import jax
import jax.numpy as jnp
from jax import lax
from jax.experimental import pallas as pl
from jax.experimental.pallas import tpu as pltpu
from jax.sharding import PartitionSpec as P

EPSILON = 1e-06
EXACT = lax.Precision.HIGHEST
F32 = jnp.float32
LANES = 128
HALF = 8
STEPS = 4


def exact_dot(a, b):
    return jnp.dot(a, b, precision=EXACT, preferred_element_type=F32)


def iota(shape, dim):
    return lax.broadcasted_iota(jnp.int32, shape, dim)


def get_rows(ref, per, row, base=0):
    if per >= HALF:
        return ref[row // per, base + row % per : base + row % per + HALF, :]
    parts = [ref[row // per + s, base : base + per, :] for s in range(HALF // per)]
    return jnp.concatenate(parts, axis=0)


def put_rows(ref, per, row, block, base=0):
    if per >= HALF:
        ref[row // per, base + row % per : base + row % per + HALF, :] = block
    else:
        for s in range(HALF // per):
            ref[row // per + s, base : base + per, :] = block[s * per : (s + 1) * per]


def member_sums(first, second, members):
    groups = LANES // members
    lane, slot = iota((LANES, LANES), 0), iota((LANES, LANES), 1)
    pick = (slot == lane // members).astype(F32)
    pick_two = (slot == groups + lane // members).astype(F32)
    return exact_dot(first, pick) + exact_dot(second, pick_two)


def state_kernel(dims, k_ref, v_ref, rate_ref, res_ref, u_ref, a_ref, r_ref, d_ref, send_ref, tab):
    tokens, tiles, modes, members, per = dims
    groups = LANES // members

    def expand(ref, out, fn):
        for j in range(tiles):
            g, lane = iota((ref.shape[1], LANES), 0), iota((ref.shape[1], LANES), 1)
            pick = (g == groups * j + lane // members).astype(F32)
            tab[pl.ds(j, modes, stride=tiles), :] = exact_dot(ref[...], pick)

    expand(res_ref, None, None)
    r_ref[...] = tab[...]
    expand(rate_ref, None, None)
    rate = jnp.exp(tab[...])
    a_ref[...] = jnp.exp(-rate)
    tab[...] = jnp.exp(-rate * float(tokens))
    for row in range(0, modes * tiles, HALF):
        put_rows(d_ref, per, row, tab[row : row + HALF, :])

    def fill(b, _):
        rows = pl.ds(pl.multiple_of(b * 16, 16), 16)
        for j in range(tiles):
            cols = slice(j * LANES, (j + 1) * LANES)
            u = k_ref[rows, cols].astype(F32) * v_ref[rows, cols].astype(F32)
            u_ref[pl.ds(b * 16 * tiles + j, 16, stride=tiles), :] = u
        return 0

    lax.fori_loop(0, tokens // 16, fill, 0)

    span = modes // 2
    zero = jnp.zeros((HALF, LANES), F32)
    for h in range(0, tiles, HALF):
        for first in range(0, modes, span):
            rows = [(first + i) * tiles + h for i in range(span)]
            a = [a_ref[row : row + HALF, :] for row in rows]

            def step(n, carry):
                hs, ms = carry
                for s in range(STEPS):
                    t = n * STEPS + s
                    u = u_ref[pl.ds(pl.multiple_of(t * tiles + h, HALF), HALF), :]
                    aged = [x * y for x, y in zip(a, hs)]
                    ms = [x * m + y for x, m, y in zip(a, ms, aged)]
                    hs = [y + u for y in aged]
                return tuple(hs), tuple(ms)

            hs, ms = lax.fori_loop(0, tokens // STEPS, step, ((zero,) * span, (zero,) * span))
            for i, row in enumerate(rows):
                put_rows(send_ref, per, row, hs[i])
                put_rows(send_ref, per, row, ms[i], base=per)


def prefix_kernel(per, got_ref, d_ref, both_ref, send_ref):
    count = got_ref.shape[0]
    decay = d_ref[lax.axis_index("ctx")]
    decay = jnp.concatenate([decay, decay], axis=0)

    def step(i, before):
        both_ref[i] = before
        send_ref[i] = before[:per]
        return decay * before + got_ref[i]

    lax.fori_loop(0, count, step, jnp.zeros(decay.shape, F32), unroll=8)


def mix_kernel(
    dims, u_ref, gate_ref, cot_ref, skip_ref, gain_ref, a_ref, r_ref, in_ref, mixed_ref, sums_ref, y_ref, acc_ref
):
    tokens, tiles, modes, members, per = dims
    for h in range(0, tiles, HALF):
        rows = [i * tiles + h for i in range(modes)]
        a = [a_ref[row : row + HALF, :] for row in rows]
        res = [r_ref[row : row + HALF, :] for row in rows]

        def step(n, hs):
            for s in range(STEPS):
                at = pl.ds(pl.multiple_of((n * STEPS + s) * tiles + h, HALF), HALF)
                u = u_ref[at, :]
                hs = [x * y + u for x, y in zip(a, hs)]
                y = [x * z for x, z in zip(res, hs)]
                while len(y) > 1:
                    y = [y[i] + y[i + 1] for i in range(0, len(y), 2)]
                y_ref[at, :] = y[0]
            return tuple(hs)

        start = tuple(get_rows(in_ref, per, row) for row in rows)
        lax.fori_loop(0, tokens // STEPS, step, start)

    def block(b, _):
        rows = pl.ds(pl.multiple_of(b * 16, 16), 16)
        squares = jnp.zeros((16, LANES), F32)
        inner = jnp.zeros((16, LANES), F32)
        for j in range(tiles):
            cols = slice(j * LANES, (j + 1) * LANES)
            at = pl.ds(b * 16 * tiles + j, 16, stride=tiles)
            mixed = y_ref[at, :] + skip_ref[:, cols] * u_ref[at, :]
            mixed_ref[rows, cols] = mixed
            premix = gate_ref[rows, cols].astype(F32) * mixed
            pull = cot_ref[rows, cols].astype(F32) * gain_ref[:, cols]
            squares = squares + premix * premix
            inner = inner + pull * premix
        acc_ref[0, rows, :] = squares
        acc_ref[1, rows, :] = inner
        return 0

    lax.fori_loop(0, tokens // 16, block, 0)
    for s in range(2):
        sums_ref[s : s + 1, :] = jnp.sum(acc_ref[s].T, axis=0, keepdims=True)


def norm_kernel(
    dims, width, sums_ref, mixed_ref, u_ref, gate_ref, cot_ref, gain_ref, a_ref, in_ref,
    out_ref, grad_q_ref, w_ref, send_ref, row_ref, part_ref,
):
    tokens, tiles, modes, members, per = dims
    total = jnp.sum(sums_ref[...], axis=0)
    inverse = lax.rsqrt(total[0:1] / width + EPSILON)
    inner = inverse * total[1:2] / width
    row_ref[0] = jnp.broadcast_to(inverse, (LANES, tokens)).T
    row_ref[1] = jnp.broadcast_to(inner, (LANES, tokens)).T

    def block(b, _):
        rows = pl.ds(pl.multiple_of(b * 16, 16), 16)
        inverse, inner = row_ref[0, rows, :], row_ref[1, rows, :]
        for j in range(tiles):
            cols = slice(j * LANES, (j + 1) * LANES)
            mixed = mixed_ref[rows, cols]
            gate = gate_ref[rows, cols].astype(F32)
            gain = gain_ref[:, cols]
            normed = gate * mixed * inverse
            out_ref[rows, cols] = (normed * gain).astype(jnp.bfloat16)
            pull = cot_ref[rows, cols].astype(F32) * gain
            dpre = (pull - normed * inner) * inverse
            grad_q_ref[rows, cols] = (dpre * mixed).astype(jnp.bfloat16)
            w_ref[pl.ds(b * 16 * tiles + j, 16, stride=tiles), :] = dpre * gate
        return 0

    lax.fori_loop(0, tokens // 16, block, 0)

    span = modes // 2
    zero = jnp.zeros((HALF, LANES), F32)
    for h in range(0, tiles, HALF):
        for first in range(0, modes, span):
            rows = [(first + i) * tiles + h for i in range(span)]
            a = [a_ref[row : row + HALF, :] for row in rows]

            def step(n, carry):
                xs, ms, res, mom = carry
                for s in range(STEPS):
                    t = tokens - 1 - (n * STEPS + s)
                    at = pl.ds(pl.multiple_of(t * tiles + h, HALF), HALF)
                    w, u = w_ref[at, :], u_ref[at, :]
                    bs = [x + w for x in xs]
                    ms = [y * m + x for y, m, x in zip(a, ms, xs)]
                    xs = [y * b for y, b in zip(a, bs)]
                    res = [p + u * b for p, b in zip(res, bs)]
                    mom = [p + u * m for p, m in zip(mom, ms)]
                return tuple(xs), tuple(ms), tuple(res), tuple(mom)

            xs, ms, res, mom = lax.fori_loop(0, tokens // STEPS, step, ((zero,) * span,) * 4)
            for i, row in enumerate(rows):
                put_rows(send_ref, per, row, xs[i])
                part_ref[0, row : row + HALF, :] = res[i]
                lead_moment = a[i] * ms[i] + xs[i]
                part_ref[1, row : row + HALF, :] = mom[i] + lead_moment * get_rows(in_ref, per, row)
    part_ref[0] = member_sums(part_ref[0], part_ref[1], members)
    for row in range(0, modes * tiles, HALF):
        put_rows(send_ref, per, row, part_ref[0, row : row + HALF, :], base=per)


def suffix_kernel(dims, got_ref, both_ref, d_ref, send_ref):
    tokens, tiles, modes, members, per = dims
    count = got_ref.shape[0]
    decay = d_ref[lax.axis_index("ctx")]
    zero = jnp.zeros((per, LANES), F32)

    def step(n, carry):
        after, part, res, mom = carry
        i = count - 1 - n
        got, both = got_ref[i], both_ref[i]
        lead, before, moment = got[:per], both[:per], both[per:]
        send_ref[i, :per, :] = after
        aged = decay * after
        part = part + got[per:]
        res = res + lead * before
        mom = mom + lead * moment + float(tokens) * aged * before
        return aged + lead, part, res, mom

    _, part, res, mom = lax.fori_loop(0, count, step, (zero,) * 4, unroll=8)
    pad = max(HALF - per, 0)
    if pad:
        fill = jnp.zeros((pad, LANES), F32)
        res, mom = jnp.concatenate([res, fill], axis=0), jnp.concatenate([mom, fill], axis=0)
    part = part + member_sums(res, mom, members)[:per]

    def spread(i, _):
        send_ref[i, per:, :] = part
        return 0

    lax.fori_loop(0, count, spread, 0, unroll=8)


def grad_kernel(
    dims, total_tokens, got_ref, w_ref, k_ref, v_ref, skip_ref, a_ref, r_ref, residue_ref, log_ref,
    grad_k_ref, grad_v_ref, grad_res_ref, grad_log_ref, y_ref, tot_ref,
):
    tokens, tiles, modes, members, per = dims
    for h in range(0, tiles, HALF):
        rows = [i * tiles + h for i in range(modes)]
        a = [a_ref[row : row + HALF, :] for row in rows]
        res = [r_ref[row : row + HALF, :] for row in rows]

        def step(n, xs):
            for s in range(STEPS):
                t = tokens - 1 - (n * STEPS + s)
                at = pl.ds(pl.multiple_of(t * tiles + h, HALF), HALF)
                w = w_ref[at, :]
                bs = [x + w for x in xs]
                xs = [y * b for y, b in zip(a, bs)]
                y = [x * z for x, z in zip(res, bs)]
                while len(y) > 1:
                    y = [y[i] + y[i + 1] for i in range(0, len(y), 2)]
                y_ref[at, :] = y[0]
            return tuple(xs)

        start = tuple(get_rows(got_ref, per, row) for row in rows)
        lax.fori_loop(0, tokens // STEPS, step, start)

    def block(b, _):
        rows = pl.ds(pl.multiple_of(b * 16, 16), 16)
        for j in range(tiles):
            cols = slice(j * LANES, (j + 1) * LANES)
            at = pl.ds(b * 16 * tiles + j, 16, stride=tiles)
            grad = y_ref[at, :] + skip_ref[:, cols] * w_ref[at, :]
            grad_k_ref[rows, cols] = (grad * v_ref[rows, cols].astype(F32)).astype(jnp.bfloat16)
            grad_v_ref[rows, cols] = (grad * k_ref[rows, cols].astype(F32)).astype(jnp.bfloat16)
        return 0

    lax.fori_loop(0, tokens // 16, block, 0)

    for row in range(0, modes * tiles, HALF):
        tot_ref[row : row + HALF, :] = get_rows(got_ref, per, row, base=per)
    group_tile = LANES // members
    states, groups = modes * tiles, residue_ref.shape[0]
    slot, group = iota((LANES, groups), 0), iota((LANES, groups), 1)
    own = iota((states, groups), 0) % tiles == iota((states, groups), 1) // group_tile
    mode_of = (iota((LANES, states), 1) // tiles == iota((LANES, states), 0)).astype(F32)
    sums = []
    for s in range(2):
        pick = (slot == s * group_tile + group % group_tile).astype(F32)
        spread = jnp.where(own, exact_dot(tot_ref[...], pick), 0.0)
        sums.append(exact_dot(mode_of, spread).T[:, :modes] / total_tokens)
    grad_res_ref[...] = sums[0]
    grad_log_ref[...] = -residue_ref[...] * jnp.exp(log_ref[...]) * sums[1]


def call(kernel, name, outs, scratch=()):
    vmem = pl.BlockSpec(memory_space=pltpu.VMEM)
    return lambda *args: pl.pallas_call(
        kernel,
        name=name,
        out_shape=[jax.ShapeDtypeStruct(s, d) for s, d in outs],
        in_specs=[vmem] * len(args),
        out_specs=[vmem] * len(outs),
        scratch_shapes=[pltpu.VMEM(s, F32) for s in scratch],
    )(*args)


def per_device(out_gate, key_proj, value_proj, residue, log_decay, skip, gain, cotangent):
    tokens, channels = out_gate.shape
    groups, modes = residue.shape
    members, tiles = channels // groups, channels // LANES
    shards = lax.axis_size("ctx")
    width = float(channels * lax.axis_size("tp"))
    states = modes * tiles
    per = states // shards
    dims = (tokens, tiles, modes, members, per)
    bf16 = jnp.bfloat16
    flat, state = ((tokens * tiles, LANES), F32), ((states, LANES), F32)
    one, two = ((shards, per, LANES), F32), ((shards, 2 * per, LANES), F32)
    narrow = ((tokens, channels), bf16)
    skip, gain = skip[None], gain[None]

    def exchange(value):
        return lax.all_to_all(value, "ctx", 0, 0, tiled=True)

    u, a, r, d, send = call(
        functools.partial(state_kernel, dims), "state", [flat, state, state, one, two], [state[0]]
    )(key_proj, value_proj, log_decay.T, residue.T)
    both, send = call(functools.partial(prefix_kernel, per), "prefix", [two, one])(exchange(send), d)
    before = exchange(send)
    mixed, sums = call(
        functools.partial(mix_kernel, dims),
        "mix",
        [((tokens, channels), F32), ((2, tokens), F32)],
        [flat[0], (2, tokens, LANES)],
    )(u, out_gate, cotangent, skip, gain, a, r, before)
    sums = lax.all_gather(sums, "tp")
    mixer_out, grad_q, w, send = call(
        functools.partial(norm_kernel, dims, width),
        "norm",
        [narrow, narrow, flat, two],
        [(2, tokens, LANES), (2, states, LANES)],
    )(sums, mixed, u, out_gate, cotangent, gain, a, before)
    (send,) = call(functools.partial(suffix_kernel, dims), "suffix", [two])(exchange(send), both, d)
    grad_k, grad_v, grad_residue, grad_log_decay = call(
        functools.partial(grad_kernel, dims, float(tokens * shards)),
        "grad",
        [narrow, narrow, ((groups, modes), F32), ((groups, modes), F32)],
        [flat[0], state[0]],
    )(exchange(send), w, key_proj, value_proj, skip, a, r, residue, log_decay)
    return (mixer_out, grad_q, grad_k, grad_v, grad_residue, grad_log_decay)


def solution(mesh):
    tokens, split = P("ctx", "tp"), P("tp", None)
    return jax.shard_map(
        per_device,
        mesh=mesh,
        in_specs=(tokens, tokens, tokens, split, split, P("tp"), P("tp"), tokens),
        out_specs=(tokens, tokens, tokens, tokens, split, split),
        check_vma=False,
    )
```

```python
import functools

import jax
import jax.numpy as jnp
from jax import lax
from jax.experimental import pallas as pl
from jax.experimental.pallas import tpu as pltpu
from jax.sharding import PartitionSpec as P

EPSILON = 1e-06
F32 = jnp.float32
LANES = 128
HALF = 8
STEPS = 8
BLOCK = 16


def iota(shape, dim):
    return lax.broadcasted_iota(jnp.int32, shape, dim)


def get_rows(ref, per, row, base=0):
    if per >= HALF:
        return ref[row // per, base + row % per : base + row % per + HALF, :]
    parts = [ref[row // per + s, base : base + per, :] for s in range(HALF // per)]
    return jnp.concatenate(parts, axis=0)


def put_rows(ref, per, row, block, base=0):
    if per >= HALF:
        ref[row // per, base + row % per : base + row % per + HALF, :] = block
    else:
        for s in range(HALF // per):
            ref[row // per + s, base : base + per, :] = block[s * per : (s + 1) * per]


def member_sums(first, second, members):
    groups = LANES // members
    shift = 1
    while shift < members:
        first = first + pltpu.roll(first, LANES - shift, 1)
        second = second + pltpu.roll(second, LANES - shift, 1)
        shift *= 2
    lane = iota(first.shape, 1)
    at = (lane % groups) * members
    first = jnp.take_along_axis(first, at, axis=1)
    second = jnp.take_along_axis(second, at, axis=1)
    return jnp.where(lane < groups, first, second)


def expand(ref, out, tiles, members):
    modes = ref.shape[0]
    value = ref[...]
    lane = iota(value.shape, 1)
    for j in range(tiles):
        at = (LANES // members) * j + lane // members
        out[pl.ds(j, modes, stride=tiles), :] = jnp.take_along_axis(value, at, axis=1)


def tree_sum(parts):
    while len(parts) > 1:
        parts = [sum(parts[i : i + 2]) for i in range(0, len(parts), 2)]
    return parts[0]


def tile(t, tiles, h):
    return pl.ds(pl.multiple_of(t * tiles + h, HALF), HALF)


def build_powers(first, factor_ref, out_ref):
    for row in range(0, factor_ref.shape[0], HALF):
        factor = factor_ref[row : row + HALF, :]
        value = jnp.ones_like(factor) if first is None else first[row : row + HALF, :]
        for i in range(BLOCK + 1):
            out_ref[i, row : row + HALF, :] = value
            if i < BLOCK:
                value = value * factor


def block_power(a_ref, out_ref):
    for row in range(0, a_ref.shape[0], HALF):
        value, n = a_ref[row : row + HALF, :], 1
        while n < BLOCK:
            value, n = value * value, 2 * n
        out_ref[row : row + HALF, :] = value


def fetch(pairs, sem, base=0):
    copies = [pltpu.make_async_copy(a, b, sem.at[base + i]) for i, (a, b) in enumerate(pairs)]
    for copy in copies:
        copy.start()
    return copies


def send_part(send_ref, send_hbm, sem, dims, first, span):
    tokens, tiles, modes, members, per = dims
    pieces = pl.ds(first * tiles // per, span * tiles // per)
    return fetch([(send_ref.at[pieces], send_hbm.at[pieces])], sem, first // span)


def state_kernel(
    dims, k_hbm, v_hbm, log_hbm, u_ref, a_ref, d_ref, send_hbm,
    k_ref, v_ref, log_ref, tab, power_ref, send_ref, sem, out_sem,
):
    tokens, tiles, modes, members, per = dims
    chunks = 4
    size = tokens // chunks
    (pull,) = fetch([(log_hbm, log_ref)], sem)
    copies = []
    for c in range(chunks):
        rows = pl.ds(c * size, size)
        pairs = [(k_hbm.at[rows, :], k_ref.at[rows, :]), (v_hbm.at[rows, :], v_ref.at[rows, :])]
        copies.append(fetch(pairs, sem, 1 + 2 * c))
    pull.wait()
    expand(log_ref, tab, tiles, members)
    for row in range(0, modes * tiles, HALF):
        rate = jnp.exp(tab[row : row + HALF, :])
        a_ref[row : row + HALF, :] = jnp.exp(-rate)
        put_rows(d_ref, per, row, jnp.exp(-rate * float(tokens)))
    build_powers(None, a_ref, power_ref)

    def fill(b, _):
        rows = pl.ds(pl.multiple_of(b * 16, 16), 16)
        for j in range(tiles):
            cols = slice(j * LANES, (j + 1) * LANES)
            u = k_ref[rows, cols].astype(F32) * v_ref[rows, cols].astype(F32)
            u_ref[pl.ds(b * 16 * tiles + j, 16, stride=tiles), :] = u
        return 0

    for c, pair in enumerate(copies):
        for copy in pair:
            copy.wait()
        lax.fori_loop(c * size // 16, (c + 1) * size // 16, fill, 0)

    span = modes // 2
    zero = jnp.zeros((HALF, LANES), F32)
    out = []
    for first in range(0, modes, span):
        for h in range(0, tiles, HALF):
            rows = [(first + i) * tiles + h for i in range(span)]

            def step(n, carry):
                hs, ms = carry
                xs = mx = None
                for i in range(BLOCK):
                    u = u_ref[tile(n * BLOCK + i, tiles, h), :]
                    if i == BLOCK - 1:
                        xs = [x + u for x in xs]
                        break
                    now = [power_ref[BLOCK - 1 - i, row : row + HALF, :] * u for row in rows]
                    xs = now if xs is None else [x + y for x, y in zip(xs, now)]
                    mx = xs if mx is None else [m + x for m, x in zip(mx, xs)]
                ends = [power_ref[BLOCK, row : row + HALF, :] for row in rows]
                ms = [e * (m + BLOCK * y) + x for e, m, y, x in zip(ends, ms, hs, mx)]
                hs = [e * y + x for e, y, x in zip(ends, hs, xs)]
                return tuple(hs), tuple(ms)

            hs, ms = lax.fori_loop(0, tokens // BLOCK, step, ((zero,) * span, (zero,) * span))
            for i, row in enumerate(rows):
                put_rows(send_ref, per, row, hs[i])
                put_rows(send_ref, per, row, ms[i], base=per)
        out += send_part(send_ref, send_hbm, out_sem, dims, first, span)
    for copy in out:
        copy.wait()


def local_kernel(
    dims, u_ref, a_ref, res_ref, r_ref, u_hbm, y_hbm, start_hbm, moment_hbm, y_ref, start_ref, moment_ref, sem
):
    tokens, tiles, modes, members, per = dims
    copies = fetch([(u_ref, u_hbm)], sem)
    expand(res_ref, r_ref, tiles, members)
    span = modes // 2
    zero = jnp.zeros((HALF, LANES), F32)
    for h in range(0, tiles, HALF):
        for first in range(0, modes, span):
            rows = [(first + i) * tiles + h for i in range(span)]
            a = [a_ref[row : row + HALF, :] for row in rows]
            res = [r_ref[row : row + HALF, :] for row in rows]

            def step(n, carry):
                hs, ms = carry
                for i, row in enumerate(rows):
                    start_ref[n, row : row + HALF, :] = hs[i]
                    moment_ref[n, row : row + HALF, :] = ms[i]
                for s in range(BLOCK):
                    at = tile(n * BLOCK + s, tiles, h)
                    u = u_ref[at, :]
                    aged = [x * y for x, y in zip(a, hs)]
                    ms = [x * m + y for x, m, y in zip(a, ms, aged)]
                    hs = [y + u for y in aged]
                    y = tree_sum([x * z for x, z in zip(res, hs)])
                    y_ref[at, :] = y_ref[at, :] + y if first else y
                return tuple(hs), tuple(ms)

            lax.fori_loop(0, tokens // BLOCK, step, ((zero,) * span, (zero,) * span))
    copies += fetch([(y_ref, y_hbm), (start_ref, start_hbm), (moment_ref, moment_hbm)], sem, 1)
    for copy in copies:
        copy.wait()


def prefix_kernel(per, got_ref, d_ref, after_hbm, both_ref, send_ref):
    count = got_ref.shape[0]
    decay = d_ref[lax.axis_index("ctx")]
    decay = jnp.concatenate([decay, decay], axis=0)

    def step(i, before):
        both_ref[i] = before
        send_ref[i] = before[:per]
        return decay * before + got_ref[i]

    lax.fori_loop(0, count, step, jnp.zeros(decay.shape, F32), unroll=8)


def age_states(dims, in_ref, end_ref, aged_ref):
    tokens, tiles, modes, members, per = dims
    for row in range(0, modes * tiles, HALF):
        state = get_rows(in_ref, per, row)
        for n in range(tokens // BLOCK):
            aged_ref[n, row : row + HALF, :] = state
            if n + 1 < tokens // BLOCK:
                state = state * end_ref[row : row + HALF, :]


def add_arrived(dims, aged_ref, taps_ref, y_ref, forward):
    tokens, tiles, modes, members, per = dims
    for h in range(0, tiles, HALF):
        rows = [i * tiles + h for i in range(modes)]

        def step(i, _):
            taps = [taps_ref[i + 1 if forward else i, row : row + HALF, :] for row in rows]
            for n in range(tokens // BLOCK):
                t = n * BLOCK + i
                at = tile(t if forward else tokens - 1 - t, tiles, h)
                parts = [x * aged_ref[n, row : row + HALF, :] for x, row in zip(taps, rows)]
                y_ref[at, :] = y_ref[at, :] + tree_sum(parts)
            return 0

        lax.fori_loop(0, BLOCK, step, 0)


def mix_kernel(
    dims, local_hbm, u_ref, gate_hbm, cot_hbm, skip_hbm, gain_hbm, a_ref, r_ref, in_ref, mixed_ref, sums_ref,
    gate_ref, cot_ref, skip_ref, gain_ref, power_ref, taps_ref, aged_ref, y_ref, acc_ref, sem,
):
    tokens, tiles, modes, members, per = dims
    copies = fetch(
        [(local_hbm, y_ref), (gate_hbm, gate_ref), (cot_hbm, cot_ref), (skip_hbm, skip_ref), (gain_hbm, gain_ref)], sem
    )
    build_powers(r_ref, a_ref, taps_ref)
    block_power(a_ref, power_ref)
    age_states(dims, in_ref, power_ref, aged_ref)
    copies[0].wait()
    add_arrived(dims, aged_ref, taps_ref, y_ref, True)
    for copy in copies[1:]:
        copy.wait()

    def block(b, _):
        rows = pl.ds(pl.multiple_of(b * 16, 16), 16)
        squares = jnp.zeros((16, LANES), F32)
        inner = jnp.zeros((16, LANES), F32)
        for j in range(tiles):
            cols = slice(j * LANES, (j + 1) * LANES)
            at = pl.ds(b * 16 * tiles + j, 16, stride=tiles)
            mixed = y_ref[at, :] + skip_ref[:, cols] * u_ref[at, :]
            mixed_ref[rows, cols] = mixed
            premix = gate_ref[rows, cols].astype(F32) * mixed
            pull = cot_ref[rows, cols].astype(F32) * gain_ref[:, cols]
            squares = squares + premix * premix
            inner = inner + pull * premix
        acc_ref[0, rows, :] = squares
        acc_ref[1, rows, :] = inner
        return 0

    lax.fori_loop(0, tokens // 16, block, 0)
    for s in range(2):
        sums_ref[s : s + 1, :] = jnp.sum(acc_ref[s].T, axis=0, keepdims=True)


def norm_kernel(
    dims, width, sums_ref, mixed_ref, gate_ref, cot_ref, gain_ref, a_ref, in_ref, u_hbm, start_hbm, moment_hbm,
    w_ref, send_hbm, row_hbm, row_ref, send_ref, u_ref, start_ref, moment_ref, power_ref, aged_ref, part_ref, sem, out_sem,
):
    tokens, tiles, modes, members, per = dims
    copies = fetch([(u_hbm, u_ref), (start_hbm, start_ref), (moment_hbm, moment_ref)], sem)
    total = jnp.sum(sums_ref[...], axis=0)
    inverse = lax.rsqrt(total[0:1] / width + EPSILON)
    inner = inverse * total[1:2] / width
    row_ref[0] = jnp.broadcast_to(inverse, (LANES, tokens)).T
    row_ref[1] = jnp.broadcast_to(inner, (LANES, tokens)).T
    save = fetch([(row_ref, row_hbm)], out_sem, 2)

    def block(b, _):
        rows = pl.ds(pl.multiple_of(b * 16, 16), 16)
        inverse, inner = row_ref[0, rows, :], row_ref[1, rows, :]
        for j in range(tiles):
            cols = slice(j * LANES, (j + 1) * LANES)
            gate = gate_ref[rows, cols].astype(F32)
            normed = gate * mixed_ref[rows, cols] * inverse
            pull = cot_ref[rows, cols].astype(F32) * gain_ref[:, cols]
            dpre = (pull - normed * inner) * inverse
            w_ref[pl.ds(b * 16 * tiles + j, 16, stride=tiles), :] = dpre * gate
        return 0

    lax.fori_loop(0, tokens // 16, block, 0)

    build_powers(None, a_ref, power_ref)
    age_states(dims, in_ref, power_ref.at[BLOCK], aged_ref)
    copies[0].wait()

    blocks = tokens // BLOCK
    zero = jnp.zeros((HALF, LANES), F32)
    for h in range(0, tiles, HALF):

        def pairs(n, lags):
            lags = list(lags)
            us = []
            for i in range(BLOCK):
                at = tile(n * BLOCK + i, tiles, h)
                us.append(u_ref[at, :])
                w = w_ref[at, :]
                for lag in range(i + 1):
                    lags[lag] = lags[lag] + w * us[i - lag]
            return tuple(lags)

        lags = lax.fori_loop(0, blocks, pairs, (zero,) * BLOCK)
        scaled = [lag * float(i) for i, lag in enumerate(lags)]
        for r in range(modes):
            row = r * tiles + h
            decay = power_ref[1, row : row + HALF, :]
            first, second = lags[-1], scaled[-1]
            for i in range(BLOCK - 2, -1, -1):
                first = first * decay + lags[i]
                second = second * decay + scaled[i] if i else second * decay
            part_ref[0, row : row + HALF, :] = first
            part_ref[1, row : row + HALF, :] = second

    copies[1].wait()
    copies[2].wait()

    span = modes // 2
    out = []
    for first in range(0, modes, span):
        for h in range(0, tiles, HALF):
            rows = [(first + i) * tiles + h for i in range(span)]

            def step(m, carry):
                lead, res, mom = carry
                n = blocks - 1 - m
                xs = mx = None
                for i in range(BLOCK - 1, -1, -1):
                    w = w_ref[tile(n * BLOCK + i, tiles, h), :]
                    now = [power_ref[i + 1, row : row + HALF, :] * w for row in rows]
                    xs = now if xs is None else [x + y for x, y in zip(xs, now)]
                    mx = xs if mx is None else [x + y for x, y in zip(mx, xs)]
                aged = [aged_ref[n, row : row + HALF, :] for row in rows]
                states = [start_ref[n, row : row + HALF, :] + g for row, g in zip(rows, aged)]
                age = (n * BLOCK).astype(F32)
                moments = [moment_ref[n, row : row + HALF, :] + age * g for row, g in zip(rows, aged)]
                lead = [power_ref[BLOCK, row : row + HALF, :] * y + x for row, y, x in zip(rows, lead, xs)]
                res = [p + x * s for p, x, s in zip(res, xs, states)]
                mom = [p + y * s + x * t for p, y, s, x, t in zip(mom, mx, states, xs, moments)]
                return tuple(lead), tuple(res), tuple(mom)

            start = (
                (zero,) * span,
                tuple(part_ref[0, row : row + HALF, :] for row in rows),
                tuple(part_ref[1, row : row + HALF, :] for row in rows),
            )
            lead, res, mom = lax.fori_loop(0, blocks, step, start)
            for i, row in enumerate(rows):
                put_rows(send_ref, per, row, lead[i])
                put_rows(send_ref, per, row, member_sums(res[i], mom[i], members), base=per)
        out += send_part(send_ref, send_hbm, out_sem, dims, first, span)
    for copy in save + out:
        copy.wait()


def back_kernel(dims, row_ref, mixed_ref, gate_ref, cot_ref, gain_ref, w_ref, a_ref, r_ref, out_ref, grad_q_ref, y_ref):
    tokens, tiles, modes, members, per = dims

    def block(b, _):
        rows = pl.ds(pl.multiple_of(b * 16, 16), 16)
        inverse, inner = row_ref[0, rows, :], row_ref[1, rows, :]
        for j in range(tiles):
            cols = slice(j * LANES, (j + 1) * LANES)
            mixed = mixed_ref[rows, cols]
            gain = gain_ref[:, cols]
            normed = gate_ref[rows, cols].astype(F32) * mixed * inverse
            out_ref[rows, cols] = (normed * gain).astype(jnp.bfloat16)
            pull = cot_ref[rows, cols].astype(F32) * gain
            dpre = (pull - normed * inner) * inverse
            grad_q_ref[rows, cols] = (dpre * mixed).astype(jnp.bfloat16)
        return 0

    lax.fori_loop(0, tokens // 16, block, 0)
    zero = jnp.zeros((HALF, LANES), F32)
    for h in range(0, tiles, HALF):
        rows = [i * tiles + h for i in range(modes)]
        a = [a_ref[row : row + HALF, :] for row in rows]
        res = [r_ref[row : row + HALF, :] for row in rows]

        def step(n, xs):
            for s in range(STEPS):
                at = tile(tokens - 1 - (n * STEPS + s), tiles, h)
                w = w_ref[at, :]
                bs = [x + w for x in xs]
                xs = [y * b for y, b in zip(a, bs)]
                y_ref[at, :] = tree_sum([x * z for x, z in zip(res, bs)])
            return tuple(xs)

        lax.fori_loop(0, tokens // STEPS, step, (zero,) * modes)


def suffix_kernel(dims, got_ref, both_ref, d_ref, after_hbm, send_ref):
    tokens, tiles, modes, members, per = dims
    count = got_ref.shape[0]
    decay = d_ref[lax.axis_index("ctx")]
    zero = jnp.zeros((per, LANES), F32)

    def step(n, carry):
        after, part, mom = carry
        i = count - 1 - n
        got, both = got_ref[i], both_ref[i]
        lead, before, moment = got[:per], both[:per], both[per:]
        send_ref[i, :per, :] = after
        aged = decay * after
        part = part + got[per:]
        mom = mom + lead * moment + float(tokens) * aged * before
        return aged + lead, part, mom

    _, part, mom = lax.fori_loop(0, count, step, (zero,) * 3, unroll=8)
    pad = max(HALF - per, 0)
    if pad:
        mom = jnp.concatenate([mom, jnp.zeros((pad, LANES), F32)], axis=0)
    part = part + member_sums(jnp.zeros_like(mom), mom, members)[:per]

    def spread(i, _):
        send_ref[i, per:, :] = part
        return 0

    lax.fori_loop(0, count, spread, 0, unroll=8)


def grad_kernel(
    dims, total_tokens, got_ref, local_hbm, w_ref, k_hbm, v_hbm, skip_hbm, a_ref, r_ref, residue_hbm, log_hbm,
    grad_k_ref, grad_v_ref, grad_res_ref, grad_log_ref,
    k_ref, v_ref, skip_ref, residue_ref, log_ref, power_ref, taps_ref, aged_ref, y_ref, tot_ref, sem,
):
    tokens, tiles, modes, members, per = dims
    copies = fetch(
        [
            (local_hbm, y_ref), (k_hbm, k_ref), (v_hbm, v_ref), (skip_hbm, skip_ref),
            (residue_hbm, residue_ref), (log_hbm, log_ref),
        ],
        sem,
    )
    build_powers(r_ref, a_ref, taps_ref)
    block_power(a_ref, power_ref)
    age_states(dims, got_ref, power_ref, aged_ref)
    copies[0].wait()
    add_arrived(dims, aged_ref, taps_ref, y_ref, False)
    for copy in copies[1:]:
        copy.wait()

    def block(b, _):
        rows = pl.ds(pl.multiple_of(b * 16, 16), 16)
        for j in range(tiles):
            cols = slice(j * LANES, (j + 1) * LANES)
            at = pl.ds(b * 16 * tiles + j, 16, stride=tiles)
            grad = y_ref[at, :] + skip_ref[:, cols] * w_ref[at, :]
            grad_k_ref[rows, cols] = (grad * v_ref[rows, cols].astype(F32)).astype(jnp.bfloat16)
            grad_v_ref[rows, cols] = (grad * k_ref[rows, cols].astype(F32)).astype(jnp.bfloat16)
        return 0

    lax.fori_loop(0, tokens // 16, block, 0)

    for row in range(0, modes * tiles, HALF):
        tot_ref[row : row + HALF, :] = get_rows(got_ref, per, row, base=per)
    groups = LANES // members
    lane = iota((modes, LANES), 1)
    first = second = jnp.zeros((modes, LANES), F32)
    for j in range(tiles):
        value = tot_ref[pl.ds(j, modes, stride=tiles), :]
        own = lane // groups == j
        first = jnp.where(own, jnp.take_along_axis(value, lane % groups, axis=1), first)
        second = jnp.where(own, jnp.take_along_axis(value, groups + lane % groups, axis=1), second)
    grad_res_ref[...] = first / total_tokens
    grad_log_ref[...] = -residue_ref[...] * jnp.exp(log_ref[...]) * second / total_tokens


def call(kernel, name, outs, scratch=(), hbm=(), out_hbm=()):
    vmem, far = pl.BlockSpec(memory_space=pltpu.VMEM), pl.BlockSpec(memory_space=pltpu.HBM)

    def place(i, value):
        return pltpu.with_memory_space_constraint(value, pltpu.HBM) if i in hbm else value

    return lambda *args: pl.pallas_call(
        kernel,
        name=name,
        out_shape=[pltpu.HBM(s, d) if i in out_hbm else jax.ShapeDtypeStruct(s, d) for i, (s, d) in enumerate(outs)],
        in_specs=[far if i in hbm else vmem for i in range(len(args))],
        out_specs=[far if i in out_hbm else vmem for i in range(len(outs))],
        scratch_shapes=[pltpu.VMEM(*s) if isinstance(s, tuple) else s for s in scratch],
        compiler_params=pltpu.CompilerParams(vmem_limit_bytes=16 * 2**20),
    )(*(place(i, x) for i, x in enumerate(args)))


def per_device(out_gate, key_proj, value_proj, residue, log_decay, skip, gain, cotangent):
    tokens, channels = out_gate.shape
    groups, modes = residue.shape
    members, tiles = channels // groups, channels // LANES
    shards = lax.axis_size("ctx")
    width = float(channels * lax.axis_size("tp"))
    states = modes * tiles
    blocks = tokens // BLOCK
    per = states // shards
    dims = (tokens, tiles, modes, members, per)
    bf16 = jnp.bfloat16
    flat, state = ((tokens * tiles, LANES), F32), ((states, LANES), F32)
    powers, starts = ((BLOCK + 1, states, LANES), F32), ((blocks, states, LANES), F32)
    one, two = ((shards, per, LANES), F32), ((shards, 2 * per, LANES), F32)
    narrow, small = ((tokens, channels), bf16), ((modes, groups), F32)
    rows = ((2, tokens, LANES), F32)
    line = ((1, channels), F32)
    skip, gain = skip[None], gain[None]
    residue, log_decay = residue.T, log_decay.T

    def exchange(value):
        return lax.all_to_all(value, "ctx", 0, 0, tiled=True)

    def sems(n):
        return pltpu.SemaphoreType.DMA((n,))

    u, a, d, send = call(
        functools.partial(state_kernel, dims),
        "state",
        [flat, state, one, two],
        [narrow, narrow, small, state, powers, two, sems(9), sems(2)],
        hbm=(0, 1, 2),
        out_hbm=(3,),
    )(key_proj, value_proj, log_decay)
    got = exchange(send)
    r, far_u, local, start, moment = call(
        functools.partial(local_kernel, dims),
        "local",
        [state, flat, flat, starts, starts],
        [flat, starts, starts, sems(4)],
        out_hbm=(1, 2, 3, 4),
    )(u, a, residue)
    both, send = call(functools.partial(prefix_kernel, per), "prefix", [two, one], hbm=(2,))(got, d, start)
    before = exchange(send)
    mixed, sums = call(
        functools.partial(mix_kernel, dims),
        "mix",
        [((tokens, channels), F32), ((2, tokens), F32)],
        [narrow, narrow, line, line, state, powers, starts, flat, rows, sems(5)],
        hbm=(0, 2, 3, 4, 5),
    )(local, u, out_gate, cotangent, skip, gain, a, r, before)
    sums = lax.all_gather(sums, "tp")
    w, send, row = call(
        functools.partial(norm_kernel, dims, width),
        "norm",
        [flat, two, rows],
        [rows, two, flat, starts, starts, powers, starts, ((2, states, LANES), F32), sems(3), sems(3)],
        hbm=(7, 8, 9),
        out_hbm=(1, 2),
    )(sums, mixed, out_gate, cotangent, gain, a, before, far_u, start, moment)
    got = exchange(send)
    mixer_out, grad_q, local = call(functools.partial(back_kernel, dims), "back", [narrow, narrow, flat])(
        row, mixed, out_gate, cotangent, gain, w, a, r
    )
    (send,) = call(functools.partial(suffix_kernel, dims), "suffix", [two], hbm=(3,))(got, both, d, grad_q)
    grad_k, grad_v, grad_residue, grad_log_decay = call(
        functools.partial(grad_kernel, dims, float(tokens * shards)),
        "grad",
        [narrow, narrow, small, small],
        [narrow, narrow, line, small, small, state, powers, starts, flat, state, sems(6)],
        hbm=(1, 3, 4, 5, 8, 9),
    )(exchange(send), local, w, key_proj, value_proj, skip, a, r, residue, log_decay)
    return (mixer_out, grad_q, grad_k, grad_v, grad_residue.T, grad_log_decay.T)


def solution(mesh):
    tokens, split = P("ctx", "tp"), P("tp", None)
    return jax.shard_map(
        per_device,
        mesh=mesh,
        in_specs=(tokens, tokens, tokens, split, split, P("tp"), P("tp"), tokens),
        out_specs=(tokens, tokens, tokens, tokens, split, split),
        check_vma=False,
    )
```

```python
import functools

import jax
import jax.numpy as jnp
from jax import lax
from jax.experimental import pallas as pl
from jax.experimental.pallas import tpu as pltpu
from jax.sharding import PartitionSpec as P

EPSILON = 1e-06
F32 = jnp.float32
LANES = 128
HALF = 8
STEPS = 8
BLOCK = 16


def iota(shape, dim):
    return lax.broadcasted_iota(jnp.int32, shape, dim)


def get_rows(ref, per, row, base=0):
    if per >= HALF:
        return ref[row // per, base + row % per : base + row % per + HALF, :]
    parts = [ref[row // per + s, base : base + per, :] for s in range(HALF // per)]
    return jnp.concatenate(parts, axis=0)


def put_rows(ref, per, row, block, base=0):
    if per >= HALF:
        ref[row // per, base + row % per : base + row % per + HALF, :] = block
    else:
        for s in range(HALF // per):
            ref[row // per + s, base : base + per, :] = block[s * per : (s + 1) * per]


def member_sums(first, second, members, per):
    groups = LANES // members
    shift = 1
    while shift < members:
        first = first + pltpu.roll(first, LANES - shift, 1)
        second = second + pltpu.roll(second, LANES - shift, 1)
        shift *= 2
    row, lane = iota(first.shape, 0), iota(first.shape, 1)
    at = (lane % groups) * members
    first = jnp.take_along_axis(first, at, axis=1)
    second = jnp.take_along_axis(second, at, axis=1)
    value = jnp.where((lane // groups) % 2 == 0, first, second)
    value = jnp.where(lane // (2 * groups) == row % per, value, 0.0)
    return [jnp.sum(value[i : i + per], axis=0, keepdims=True) for i in range(0, first.shape[0], per)]


def expand(ref, out, tiles, members):
    modes = ref.shape[0]
    value = ref[...]
    lane = iota(value.shape, 1)
    for j in range(tiles):
        at = (LANES // members) * j + lane // members
        out[pl.ds(j, modes, stride=tiles), :] = jnp.take_along_axis(value, at, axis=1)


def tree_sum(parts):
    while len(parts) > 1:
        parts = [sum(parts[i : i + 2]) for i in range(0, len(parts), 2)]
    return parts[0]


def tile(t, tiles, h):
    return pl.ds(pl.multiple_of(t * tiles + h, HALF), HALF)


def build_powers(first, factor_ref, out_ref):
    for row in range(0, factor_ref.shape[0], HALF):
        factor = factor_ref[row : row + HALF, :]
        value = jnp.ones_like(factor) if first is None else first[row : row + HALF, :]
        for i in range(BLOCK + 1):
            out_ref[i, row : row + HALF, :] = value
            if i < BLOCK:
                value = value * factor


def block_power(a_ref, out_ref):
    for row in range(0, a_ref.shape[0], HALF):
        value, n = a_ref[row : row + HALF, :], 1
        while n < BLOCK:
            value, n = value * value, 2 * n
        out_ref[row : row + HALF, :] = value


def fetch(pairs, sem, base=0):
    copies = [pltpu.make_async_copy(a, b, sem.at[base + i]) for i, (a, b) in enumerate(pairs)]
    for copy in copies:
        copy.start()
    return copies


def send_part(send_ref, send_hbm, sem, dims, first, span):
    tokens, tiles, modes, members, per = dims
    pieces = pl.ds(first * tiles // per, span * tiles // per)
    return fetch([(send_ref.at[pieces], send_hbm.at[pieces])], sem, first // span)


def state_kernel(
    dims, k_hbm, v_hbm, log_hbm, u_ref, a_ref, d_ref, send_hbm,
    k_ref, v_ref, log_ref, tab, power_ref, send_ref, sem, out_sem,
):
    tokens, tiles, modes, members, per = dims
    chunks = 4
    size = tokens // chunks
    (pull,) = fetch([(log_hbm, log_ref)], sem)
    copies = []
    for c in range(chunks):
        rows = pl.ds(c * size, size)
        pairs = [(k_hbm.at[rows, :], k_ref.at[rows, :]), (v_hbm.at[rows, :], v_ref.at[rows, :])]
        copies.append(fetch(pairs, sem, 1 + 2 * c))
    pull.wait()
    expand(log_ref, tab, tiles, members)
    for row in range(0, modes * tiles, HALF):
        rate = jnp.exp(tab[row : row + HALF, :])
        a_ref[row : row + HALF, :] = jnp.exp(-rate)
        put_rows(d_ref, per, row, jnp.exp(-rate * float(tokens)))
    build_powers(None, a_ref, power_ref)

    def fill(b, _):
        rows = pl.ds(pl.multiple_of(b * 16, 16), 16)
        for j in range(tiles):
            cols = slice(j * LANES, (j + 1) * LANES)
            u = k_ref[rows, cols].astype(F32) * v_ref[rows, cols].astype(F32)
            u_ref[pl.ds(b * 16 * tiles + j, 16, stride=tiles), :] = u
        return 0

    for c, pair in enumerate(copies):
        for copy in pair:
            copy.wait()
        lax.fori_loop(c * size // 16, (c + 1) * size // 16, fill, 0)

    span = modes // 2
    zero = jnp.zeros((HALF, LANES), F32)
    out = []
    for first in range(0, modes, span):
        for h in range(0, tiles, HALF):
            rows = [(first + i) * tiles + h for i in range(span)]

            def step(n, carry):
                hs, ms = carry
                xs = mx = None
                for i in range(BLOCK):
                    u = u_ref[tile(n * BLOCK + i, tiles, h), :]
                    if i == BLOCK - 1:
                        xs = [x + u for x in xs]
                        break
                    now = [power_ref[BLOCK - 1 - i, row : row + HALF, :] * u for row in rows]
                    xs = now if xs is None else [x + y for x, y in zip(xs, now)]
                    mx = xs if mx is None else [m + x for m, x in zip(mx, xs)]
                ends = [power_ref[BLOCK, row : row + HALF, :] for row in rows]
                ms = [e * (m + BLOCK * y) + x for e, m, y, x in zip(ends, ms, hs, mx)]
                hs = [e * y + x for e, y, x in zip(ends, hs, xs)]
                return tuple(hs), tuple(ms)

            hs, ms = lax.fori_loop(0, tokens // BLOCK, step, ((zero,) * span, (zero,) * span))
            for i, row in enumerate(rows):
                put_rows(send_ref, per, row, hs[i])
                put_rows(send_ref, per, row, ms[i], base=per)
        out += send_part(send_ref, send_hbm, out_sem, dims, first, span)
    for copy in out:
        copy.wait()


def local_kernel(
    dims, u_ref, a_ref, res_ref, skip_ref, r_ref, u_hbm, y_hbm, start_hbm, moment_hbm, y_ref, start_ref, moment_ref, sem
):
    tokens, tiles, modes, members, per = dims
    copies = fetch([(u_ref, u_hbm)], sem)
    expand(res_ref, r_ref, tiles, members)
    span = modes // 2
    zero = jnp.zeros((HALF, LANES), F32)
    for h in range(0, tiles, HALF):
        for first in range(0, modes, span):
            rows = [(first + i) * tiles + h for i in range(span)]
            a = [a_ref[row : row + HALF, :] for row in rows]
            res = [r_ref[row : row + HALF, :] for row in rows]
            skip = skip_ref[h : h + HALF, :]

            def step(n, carry):
                hs, ms = carry
                for i, row in enumerate(rows):
                    start_ref[n, row : row + HALF, :] = hs[i]
                    moment_ref[n, row : row + HALF, :] = ms[i]
                for s in range(BLOCK):
                    at = tile(n * BLOCK + s, tiles, h)
                    u = u_ref[at, :]
                    aged = [x * y for x, y in zip(a, hs)]
                    ms = [x * m + y for x, m, y in zip(a, ms, aged)]
                    hs = [y + u for y in aged]
                    y = tree_sum([x * z for x, z in zip(res, hs)])
                    y_ref[at, :] = (y_ref[at, :] if first else skip * u) + y
                return tuple(hs), tuple(ms)

            lax.fori_loop(0, tokens // BLOCK, step, ((zero,) * span, (zero,) * span))
    copies += fetch([(y_ref, y_hbm), (start_ref, start_hbm), (moment_ref, moment_hbm)], sem, 1)
    for copy in copies:
        copy.wait()


def prefix_kernel(per, got_ref, d_ref, after_hbm, both_ref, send_ref):
    count = got_ref.shape[0]
    decay = d_ref[lax.axis_index("ctx")]
    decay = jnp.concatenate([decay, decay], axis=0)

    def step(i, before):
        both_ref[i] = before
        send_ref[i] = before[:per]
        return decay * before + got_ref[i]

    lax.fori_loop(0, count, step, jnp.zeros(decay.shape, F32), unroll=8)


def age_states(dims, in_ref, end_ref, aged_ref):
    tokens, tiles, modes, members, per = dims
    for row in range(0, modes * tiles, HALF):
        state = get_rows(in_ref, per, row)
        for n in range(tokens // BLOCK):
            aged_ref[n, row : row + HALF, :] = state
            if n + 1 < tokens // BLOCK:
                state = state * end_ref[row : row + HALF, :]


def add_arrived(dims, aged_ref, taps_ref, y_ref, forward):
    tokens, tiles, modes, members, per = dims
    for h in range(0, tiles, HALF):
        rows = [i * tiles + h for i in range(modes)]

        def step(i, _):
            taps = [taps_ref[i + 1 if forward else i, row : row + HALF, :] for row in rows]
            for n in range(tokens // BLOCK):
                t = n * BLOCK + i
                at = tile(t if forward else tokens - 1 - t, tiles, h)
                parts = [x * aged_ref[n, row : row + HALF, :] for x, row in zip(taps, rows)]
                y_ref[at, :] = tree_sum(parts)
            return 0

        lax.fori_loop(0, BLOCK, step, 0, unroll=2)


def mix_kernel(
    dims, local_hbm, gate_hbm, cot_hbm, gain_hbm, a_ref, r_ref, in_ref, mixed_ref, sums_ref,
    local_ref, gate_ref, cot_ref, gain_ref, power_ref, taps_ref, aged_ref, y_ref, acc_ref, sem,
):
    tokens, tiles, modes, members, per = dims
    copies = fetch(
        [(local_hbm, local_ref), (gate_hbm, gate_ref), (cot_hbm, cot_ref), (gain_hbm, gain_ref)], sem
    )
    build_powers(r_ref, a_ref, taps_ref)
    block_power(a_ref, power_ref)
    age_states(dims, in_ref, power_ref, aged_ref)
    add_arrived(dims, aged_ref, taps_ref, y_ref, True)
    for copy in copies:
        copy.wait()

    def block(b, _):
        rows = pl.ds(pl.multiple_of(b * 16, 16), 16)
        squares = jnp.zeros((16, LANES), F32)
        inner = jnp.zeros((16, LANES), F32)
        for j in range(tiles):
            cols = slice(j * LANES, (j + 1) * LANES)
            at = pl.ds(b * 16 * tiles + j, 16, stride=tiles)
            mixed = y_ref[at, :] + local_ref[at, :]
            mixed_ref[rows, cols] = mixed
            premix = gate_ref[rows, cols].astype(F32) * mixed
            pull = cot_ref[rows, cols].astype(F32) * gain_ref[:, cols]
            squares = squares + premix * premix
            inner = inner + pull * premix
        acc_ref[0, rows, :] = squares
        acc_ref[1, rows, :] = inner
        return 0

    lax.fori_loop(0, tokens // 16, block, 0)
    for s in range(2):
        sums_ref[s : s + 1, :] = jnp.sum(acc_ref[s].T, axis=0, keepdims=True)


def norm_kernel(
    dims, width, sums_ref, mixed_ref, gate_ref, cot_ref, gain_ref, a_ref, in_ref, u_hbm, start_hbm, moment_hbm,
    w_ref, send_hbm, row_hbm, row_ref, send_ref, u_ref, start_ref, moment_ref, power_ref, aged_ref, part_ref, sem, out_sem,
):
    tokens, tiles, modes, members, per = dims
    copies = fetch([(u_hbm, u_ref), (start_hbm, start_ref), (moment_hbm, moment_ref)], sem)
    total = jnp.sum(sums_ref[...], axis=0)
    inverse = lax.rsqrt(total[0:1] / width + EPSILON)
    inner = inverse * total[1:2] / width
    row_ref[0] = jnp.broadcast_to(inverse, (LANES, tokens)).T
    row_ref[1] = jnp.broadcast_to(inner, (LANES, tokens)).T
    save = fetch([(row_ref, row_hbm)], out_sem, 2)

    def block(b, _):
        rows = pl.ds(pl.multiple_of(b * 16, 16), 16)
        inverse, inner = row_ref[0, rows, :], row_ref[1, rows, :]
        for j in range(tiles):
            cols = slice(j * LANES, (j + 1) * LANES)
            gate = gate_ref[rows, cols].astype(F32)
            normed = gate * mixed_ref[rows, cols] * inverse
            pull = cot_ref[rows, cols].astype(F32) * gain_ref[:, cols]
            dpre = (pull - normed * inner) * inverse
            w_ref[pl.ds(b * 16 * tiles + j, 16, stride=tiles), :] = dpre * gate
        return 0

    lax.fori_loop(0, tokens // 16, block, 0)

    build_powers(None, a_ref, power_ref)
    age_states(dims, in_ref, power_ref.at[BLOCK], aged_ref)
    copies[0].wait()

    blocks = tokens // BLOCK
    zero = jnp.zeros((HALF, LANES), F32)
    for h in range(0, tiles, HALF):

        def pairs(n, lags):
            lags = list(lags)
            us = []
            for i in range(BLOCK):
                at = tile(n * BLOCK + i, tiles, h)
                us.append(u_ref[at, :])
                w = w_ref[at, :]
                for lag in range(i + 1):
                    lags[lag] = lags[lag] + w * us[i - lag]
            return tuple(lags)

        lags = lax.fori_loop(0, blocks, pairs, (zero,) * BLOCK)
        scaled = [lag * float(i) for i, lag in enumerate(lags)]
        for r in range(modes):
            row = r * tiles + h
            decay = power_ref[1, row : row + HALF, :]
            first, second = lags[-1], scaled[-1]
            for i in range(BLOCK - 2, -1, -1):
                first = first * decay + lags[i]
                second = second * decay + scaled[i] if i else second * decay
            part_ref[0, row : row + HALF, :] = first
            part_ref[1, row : row + HALF, :] = second

    copies[1].wait()
    copies[2].wait()

    span = modes // 2
    out = []
    for first in range(0, modes, span):
        for h in range(0, tiles, HALF):
            rows = [(first + i) * tiles + h for i in range(span)]

            def step(m, carry):
                lead, res, mom = carry
                n = blocks - 1 - m
                xs = mx = None
                for i in range(BLOCK - 1, -1, -1):
                    w = w_ref[tile(n * BLOCK + i, tiles, h), :]
                    now = [power_ref[i + 1, row : row + HALF, :] * w for row in rows]
                    xs = now if xs is None else [x + y for x, y in zip(xs, now)]
                    mx = xs if mx is None else [x + y for x, y in zip(mx, xs)]
                aged = [aged_ref[n, row : row + HALF, :] for row in rows]
                states = [start_ref[n, row : row + HALF, :] + g for row, g in zip(rows, aged)]
                age = (n * BLOCK).astype(F32)
                moments = [moment_ref[n, row : row + HALF, :] + age * g for row, g in zip(rows, aged)]
                lead = [power_ref[BLOCK, row : row + HALF, :] * y + x for row, y, x in zip(rows, lead, xs)]
                res = [p + x * s for p, x, s in zip(res, xs, states)]
                mom = [p + y * s + x * t for p, y, s, x, t in zip(mom, mx, states, xs, moments)]
                return tuple(lead), tuple(res), tuple(mom)

            start = (
                (zero,) * span,
                tuple(part_ref[0, row : row + HALF, :] for row in rows),
                tuple(part_ref[1, row : row + HALF, :] for row in rows),
            )
            lead, res, mom = lax.fori_loop(0, blocks, step, start, unroll=2)
            for i, row in enumerate(rows):
                put_rows(send_ref, per, row, lead[i])
                for s, part in enumerate(member_sums(res[i], mom[i], members, per)):
                    send_ref[row // per + s, per : per + 1, :] = part
        out += send_part(send_ref, send_hbm, out_sem, dims, first, span)
    for copy in save + out:
        copy.wait()


def back_kernel(
    dims, row_ref, mixed_ref, gate_ref, cot_ref, gain_ref, w_ref, a_ref, r_ref, skip_ref, out_ref, grad_q_ref, y_hbm,
    y_ref, sem,
):
    tokens, tiles, modes, members, per = dims

    def block(b, _):
        rows = pl.ds(pl.multiple_of(b * 16, 16), 16)
        inverse, inner = row_ref[0, rows, :], row_ref[1, rows, :]
        for j in range(tiles):
            cols = slice(j * LANES, (j + 1) * LANES)
            mixed = mixed_ref[rows, cols]
            gain = gain_ref[:, cols]
            normed = gate_ref[rows, cols].astype(F32) * mixed * inverse
            out_ref[rows, cols] = (normed * gain).astype(jnp.bfloat16)
            pull = cot_ref[rows, cols].astype(F32) * gain
            dpre = (pull - normed * inner) * inverse
            grad_q_ref[rows, cols] = (dpre * mixed).astype(jnp.bfloat16)
        return 0

    lax.fori_loop(0, tokens // 16, block, 0)
    zero = jnp.zeros((HALF, LANES), F32)
    for h in range(0, tiles, HALF):
        rows = [i * tiles + h for i in range(modes)]
        a = [a_ref[row : row + HALF, :] for row in rows]
        res = [r_ref[row : row + HALF, :] for row in rows]
        skip = skip_ref[h : h + HALF, :]

        def step(n, xs):
            for s in range(STEPS):
                at = tile(tokens - 1 - (n * STEPS + s), tiles, h)
                w = w_ref[at, :]
                bs = [x + w for x in xs]
                xs = [y * b for y, b in zip(a, bs)]
                y_ref[at, :] = tree_sum([x * z for x, z in zip(res, bs)]) + skip * w
            return tuple(xs)

        lax.fori_loop(0, tokens // STEPS, step, (zero,) * modes)
    for copy in fetch([(y_ref, y_hbm)], sem):
        copy.wait()


def suffix_kernel(dims, got_hbm, both_hbm, d_ref, after_hbm, send_ref, got_ref, both_ref, sem):
    tokens, tiles, modes, members, per = dims
    copies = fetch([(got_hbm, got_ref), (both_hbm, both_ref)], sem)
    for copy in copies:
        copy.wait()
    count = got_ref.shape[0]
    decay = d_ref[lax.axis_index("ctx")]
    zero = jnp.zeros((per, LANES), F32)

    def step(n, carry):
        after, part, mom = carry
        i = count - 1 - n
        got, both = got_ref[i], both_ref[i]
        lead, before, moment = got[:per], both[:per], both[per:]
        send_ref[i, :per, :] = after
        aged = decay * after
        part = part + got[per:]
        mom = mom + lead * moment + float(tokens) * aged * before
        return aged + lead, part, mom

    _, part, mom = lax.fori_loop(0, count, step, (zero, zero[:1], zero), unroll=8)
    pad = max(HALF - per, 0)
    if pad:
        mom = jnp.concatenate([mom, jnp.zeros((pad, LANES), F32)], axis=0)
    part = part + member_sums(jnp.zeros_like(mom), mom, members, per)[0]

    def spread(i, _):
        send_ref[i, per:, :] = part
        return 0

    lax.fori_loop(0, count, spread, 0, unroll=8)


def grad_kernel(
    dims, total_tokens, got_ref, local_hbm, k_hbm, v_hbm, a_ref, r_ref, residue_hbm, log_hbm,
    grad_k_ref, grad_v_ref, grad_res_ref, grad_log_ref,
    local_ref, k_ref, v_ref, residue_ref, log_ref, power_ref, taps_ref, aged_ref, y_ref, tot_ref, sem,
):
    tokens, tiles, modes, members, per = dims
    copies = fetch(
        [
            (local_hbm, local_ref), (k_hbm, k_ref), (v_hbm, v_ref),
            (residue_hbm, residue_ref), (log_hbm, log_ref),
        ],
        sem,
    )
    build_powers(r_ref, a_ref, taps_ref)
    block_power(a_ref, power_ref)
    age_states(dims, got_ref, power_ref, aged_ref)
    add_arrived(dims, aged_ref, taps_ref, y_ref, False)
    for copy in copies:
        copy.wait()

    def block(b, _):
        rows = pl.ds(pl.multiple_of(b * 16, 16), 16)
        for j in range(tiles):
            cols = slice(j * LANES, (j + 1) * LANES)
            at = pl.ds(b * 16 * tiles + j, 16, stride=tiles)
            grad = y_ref[at, :] + local_ref[at, :]
            grad_k_ref[rows, cols] = (grad * v_ref[rows, cols].astype(F32)).astype(jnp.bfloat16)
            grad_v_ref[rows, cols] = (grad * k_ref[rows, cols].astype(F32)).astype(jnp.bfloat16)
        return 0

    lax.fori_loop(0, tokens // 16, block, 0)

    for piece in range(modes * tiles // per):
        tot_ref[piece : piece + 1, :] = got_ref[piece, per : per + 1, :]
    groups = LANES // members
    lane = iota((modes, LANES), 1)
    first = second = jnp.zeros((modes, LANES), F32)
    for j in range(tiles):
        value = tot_ref[pl.ds(j // per, modes, stride=tiles // per), :]
        at = 2 * groups * (j % per) + lane % groups
        own = lane // groups == j
        first = jnp.where(own, jnp.take_along_axis(value, at, axis=1), first)
        second = jnp.where(own, jnp.take_along_axis(value, groups + at, axis=1), second)
    grad_res_ref[...] = first / total_tokens
    grad_log_ref[...] = -residue_ref[...] * jnp.exp(log_ref[...]) * second / total_tokens


def call(kernel, name, outs, scratch=(), hbm=(), out_hbm=()):
    vmem, far = pl.BlockSpec(memory_space=pltpu.VMEM), pl.BlockSpec(memory_space=pltpu.HBM)

    def place(i, value):
        return pltpu.with_memory_space_constraint(value, pltpu.HBM) if i in hbm else value

    return lambda *args: pl.pallas_call(
        kernel,
        name=name,
        out_shape=[pltpu.HBM(s, d) if i in out_hbm else jax.ShapeDtypeStruct(s, d) for i, (s, d) in enumerate(outs)],
        in_specs=[far if i in hbm else vmem for i in range(len(args))],
        out_specs=[far if i in out_hbm else vmem for i in range(len(outs))],
        scratch_shapes=[pltpu.VMEM(*s) if isinstance(s, tuple) else s for s in scratch],
        compiler_params=pltpu.CompilerParams(vmem_limit_bytes=16 * 2**20),
    )(*(place(i, x) for i, x in enumerate(args)))


def per_device(out_gate, key_proj, value_proj, residue, log_decay, skip, gain, cotangent):
    tokens, channels = out_gate.shape
    groups, modes = residue.shape
    members, tiles = channels // groups, channels // LANES
    shards = lax.axis_size("ctx")
    width = float(channels * lax.axis_size("tp"))
    states = modes * tiles
    blocks = tokens // BLOCK
    per = states // shards
    dims = (tokens, tiles, modes, members, per)
    bf16 = jnp.bfloat16
    flat, state = ((tokens * tiles, LANES), F32), ((states, LANES), F32)
    powers, starts = ((BLOCK + 1, states, LANES), F32), ((blocks, states, LANES), F32)
    one, two = ((shards, per, LANES), F32), ((shards, 2 * per, LANES), F32)
    one_rows = ((shards, LANES), F32)
    wide = ((shards, per + 1, LANES), F32)
    narrow, small = ((tokens, channels), bf16), ((modes, groups), F32)
    rows = ((2, tokens, LANES), F32)
    line = ((1, channels), F32)
    skip, gain = skip.reshape(tiles, LANES), gain[None]
    residue, log_decay = residue.T, log_decay.T

    def exchange(value):
        return lax.all_to_all(value, "ctx", 0, 0, tiled=True)

    def sems(n):
        return pltpu.SemaphoreType.DMA((n,))

    u, a, d, send = call(
        functools.partial(state_kernel, dims),
        "state",
        [flat, state, one, two],
        [narrow, narrow, small, state, powers, two, sems(9), sems(2)],
        hbm=(0, 1, 2),
        out_hbm=(3,),
    )(key_proj, value_proj, log_decay)
    got = exchange(send)
    r, far_u, local, start, moment = call(
        functools.partial(local_kernel, dims),
        "local",
        [state, flat, flat, starts, starts],
        [flat, starts, starts, sems(4)],
        out_hbm=(1, 2, 3, 4),
    )(u, a, residue, skip)
    both, send = call(functools.partial(prefix_kernel, per), "prefix", [two, one], hbm=(2,))(got, d, start)
    before = exchange(send)
    mixed, sums = call(
        functools.partial(mix_kernel, dims),
        "mix",
        [((tokens, channels), F32), ((2, tokens), F32)],
        [flat, narrow, narrow, line, state, powers, starts, flat, rows, sems(4)],
        hbm=(0, 1, 2, 3),
    )(local, out_gate, cotangent, gain, a, r, before)
    sums = lax.all_gather(sums, "tp")
    w, send, row = call(
        functools.partial(norm_kernel, dims, width),
        "norm",
        [flat, wide, rows],
        [rows, wide, flat, starts, starts, powers, starts, ((2, states, LANES), F32), sems(3), sems(3)],
        hbm=(7, 8, 9),
        out_hbm=(1, 2),
    )(sums, mixed, out_gate, cotangent, gain, a, before, far_u, start, moment)
    got = exchange(send)
    mixer_out, grad_q, local = call(functools.partial(back_kernel, dims), "back", [narrow, narrow, flat], [flat, sems(1)], out_hbm=(2,))(
        row, mixed, out_gate, cotangent, gain, w, a, r, skip
    )
    (send,) = call(functools.partial(suffix_kernel, dims), "suffix", [wide], [wide, two, sems(2)], hbm=(0, 1, 3))(got, both, d, grad_q)
    grad_k, grad_v, grad_residue, grad_log_decay = call(
        functools.partial(grad_kernel, dims, float(tokens * shards)),
        "grad",
        [narrow, narrow, small, small],
        [flat, narrow, narrow, small, small, state, powers, starts, flat, one_rows, sems(5)],
        hbm=(1, 2, 3, 6, 7),
    )(exchange(send), local, key_proj, value_proj, a, r, residue, log_decay)
    return (mixer_out, grad_q, grad_k, grad_v, grad_residue.T, grad_log_decay.T)


def solution(mesh):
    tokens, split = P("ctx", "tp"), P("tp", None)
    return jax.shard_map(
        per_device,
        mesh=mesh,
        in_specs=(tokens, tokens, tokens, split, split, P("tp"), P("tp"), tokens),
        out_specs=(tokens, tokens, tokens, tokens, split, split),
        check_vma=False,
    )
```

```python
import functools

import jax
import jax.numpy as jnp
from jax import lax
from jax.experimental import pallas as pl
from jax.experimental.pallas import tpu as pltpu
from jax.sharding import PartitionSpec as P

EPSILON = 1e-06
F32 = jnp.float32
LANES = 128
HALF = 8
STEPS = 8
BLOCK = 16


def iota(shape, dim):
    return lax.broadcasted_iota(jnp.int32, shape, dim)


def get_rows(ref, per, row, base=0):
    pieces = range(row // per, (row + HALF) // per)
    if len(ref.shape) == 2:
        parts = [ref[p * (per + 1) : p * (per + 1) + per, :] for p in pieces]
    else:
        parts = [ref[p, base : base + per, :] for p in pieces]
    return jnp.concatenate(parts, axis=0)


def put_rows(ref, per, row, block, base=0):
    for s in range(HALF // per):
        p, part = row // per + s, block[s * per : (s + 1) * per]
        if len(ref.shape) == 2:
            ref[p * (per + 1) : p * (per + 1) + per, :] = part
        else:
            ref[p, base : base + per, :] = part


def member_sums(first, second, members, per):
    groups = LANES // members
    shift = 1
    while shift < members:
        first = first + pltpu.roll(first, LANES - shift, 1)
        second = second + pltpu.roll(second, LANES - shift, 1)
        shift *= 2
    row, lane = iota(first.shape, 0), iota(first.shape, 1)
    at = (lane % groups) * members
    first = jnp.take_along_axis(first, at, axis=1)
    second = jnp.take_along_axis(second, at, axis=1)
    value = jnp.where((lane // groups) % 2 == 0, first, second)
    value = jnp.where(lane // (2 * groups) == row % per, value, 0.0)
    return [jnp.sum(value[i : i + per], axis=0, keepdims=True) for i in range(0, first.shape[0], per)]


def expand(ref, out, tiles, members):
    modes = ref.shape[0]
    value = ref[...]
    lane = iota(value.shape, 1)
    for j in range(tiles):
        at = (LANES // members) * j + lane // members
        out[pl.ds(j, modes, stride=tiles), :] = jnp.take_along_axis(value, at, axis=1)


def tree_sum(parts):
    while len(parts) > 1:
        parts = [sum(parts[i : i + 2]) for i in range(0, len(parts), 2)]
    return parts[0]


def tile(t, tiles, h):
    return pl.ds(pl.multiple_of(t * tiles + h, HALF), HALF)


def build_powers(first, factor_ref, out_ref):
    for row in range(0, factor_ref.shape[0], HALF):
        factor = factor_ref[row : row + HALF, :]
        value = jnp.ones_like(factor) if first is None else first[row : row + HALF, :]
        for i in range(BLOCK + 1):
            out_ref[i, row : row + HALF, :] = value
            if i < BLOCK:
                value = value * factor


def block_power(a_ref, out_ref):
    for row in range(0, a_ref.shape[0], HALF):
        value, n = a_ref[row : row + HALF, :], 1
        while n < BLOCK:
            value, n = value * value, 2 * n
        out_ref[row : row + HALF, :] = value


def fetch(pairs, sem, base=0):
    copies = [pltpu.make_async_copy(a, b, sem.at[base + i]) for i, (a, b) in enumerate(pairs)]
    for copy in copies:
        copy.start()
    return copies


def send_part(send_ref, send_hbm, sem, dims, first, span):
    tokens, tiles, modes, members, per = dims
    size = per + 1 if len(send_ref.shape) == 2 else 1
    pieces = pl.ds(first * tiles // per * size, span * tiles // per * size)
    return fetch([(send_ref.at[pieces], send_hbm.at[pieces])], sem, first // span)


def state_kernel(
    dims, k_hbm, v_hbm, log_hbm, u_ref, a_ref, d_ref, send_hbm,
    k_ref, v_ref, log_ref, tab, power_ref, send_ref, sem, out_sem,
):
    tokens, tiles, modes, members, per = dims
    chunks = 4
    size = tokens // chunks
    (pull,) = fetch([(log_hbm, log_ref)], sem)
    copies = []
    for c in range(chunks):
        rows = pl.ds(c * size, size)
        pairs = [(k_hbm.at[rows, :], k_ref.at[rows, :]), (v_hbm.at[rows, :], v_ref.at[rows, :])]
        copies.append(fetch(pairs, sem, 1 + 2 * c))
    pull.wait()
    expand(log_ref, tab, tiles, members)
    for row in range(0, modes * tiles, HALF):
        rate = jnp.exp(tab[row : row + HALF, :])
        a_ref[row : row + HALF, :] = jnp.exp(-rate)
        put_rows(d_ref, per, row, jnp.exp(-rate * float(tokens)))
    build_powers(None, a_ref, power_ref)

    def fill(b, _):
        rows = pl.ds(pl.multiple_of(b * 16, 16), 16)
        for j in range(tiles):
            cols = slice(j * LANES, (j + 1) * LANES)
            u = k_ref[rows, cols].astype(F32) * v_ref[rows, cols].astype(F32)
            u_ref[pl.ds(b * 16 * tiles + j, 16, stride=tiles), :] = u
        return 0

    for c, pair in enumerate(copies):
        for copy in pair:
            copy.wait()
        lax.fori_loop(c * size // 16, (c + 1) * size // 16, fill, 0)

    span = modes // 2
    zero = jnp.zeros((HALF, LANES), F32)
    out = []
    for first in range(0, modes, span):
        for h in range(0, tiles, HALF):
            rows = [(first + i) * tiles + h for i in range(span)]

            def step(n, carry):
                hs, ms = carry
                xs = mx = None
                for i in range(BLOCK):
                    u = u_ref[tile(n * BLOCK + i, tiles, h), :]
                    if i == BLOCK - 1:
                        xs = [x + u for x in xs]
                        break
                    now = [power_ref[BLOCK - 1 - i, row : row + HALF, :] * u for row in rows]
                    xs = now if xs is None else [x + y for x, y in zip(xs, now)]
                    mx = xs if mx is None else [m + x for m, x in zip(mx, xs)]
                ends = [power_ref[BLOCK, row : row + HALF, :] for row in rows]
                ms = [e * (m + BLOCK * y) + x for e, m, y, x in zip(ends, ms, hs, mx)]
                hs = [e * y + x for e, y, x in zip(ends, hs, xs)]
                return tuple(hs), tuple(ms)

            hs, ms = lax.fori_loop(0, tokens // BLOCK, step, ((zero,) * span, (zero,) * span))
            for i, row in enumerate(rows):
                put_rows(send_ref, per, row, hs[i])
                put_rows(send_ref, per, row, ms[i], base=per)
        out += send_part(send_ref, send_hbm, out_sem, dims, first, span)
    for copy in out:
        copy.wait()


def local_kernel(
    dims, u_ref, a_ref, res_ref, skip_ref, r_ref, u_hbm, y_hbm, start_hbm, moment_hbm, y_ref, start_ref, moment_ref, sem
):
    tokens, tiles, modes, members, per = dims
    copies = fetch([(u_ref, u_hbm)], sem)
    expand(res_ref, r_ref, tiles, members)
    span = modes // 2
    zero = jnp.zeros((HALF, LANES), F32)
    for h in range(0, tiles, HALF):
        for first in range(0, modes, span):
            rows = [(first + i) * tiles + h for i in range(span)]
            a = [a_ref[row : row + HALF, :] for row in rows]
            res = [r_ref[row : row + HALF, :] for row in rows]
            skip = skip_ref[h : h + HALF, :]

            def step(n, carry):
                hs, ms = carry
                for i, row in enumerate(rows):
                    start_ref[n, row : row + HALF, :] = hs[i]
                    moment_ref[n, row : row + HALF, :] = ms[i]
                for s in range(BLOCK):
                    at = tile(n * BLOCK + s, tiles, h)
                    u = u_ref[at, :]
                    aged = [x * y for x, y in zip(a, hs)]
                    ms = [x * m + y for x, m, y in zip(a, ms, aged)]
                    hs = [y + u for y in aged]
                    y = tree_sum([x * z for x, z in zip(res, hs)])
                    y_ref[at, :] = (y_ref[at, :] if first else skip * u) + y
                return tuple(hs), tuple(ms)

            lax.fori_loop(0, tokens // BLOCK, step, ((zero,) * span, (zero,) * span))
    copies += fetch([(y_ref, y_hbm), (start_ref, start_hbm), (moment_ref, moment_hbm)], sem, 1)
    for copy in copies:
        copy.wait()


def prefix_kernel(per, got_ref, d_ref, after_hbm, both_ref, send_ref):
    count = got_ref.shape[0]
    decay = d_ref[lax.axis_index("ctx")]
    decay = jnp.concatenate([decay, decay], axis=0)

    def step(i, before):
        both_ref[i] = before
        send_ref[i] = before[:per]
        return decay * before + got_ref[i]

    lax.fori_loop(0, count, step, jnp.zeros(decay.shape, F32), unroll=8)


def age_states(dims, in_ref, end_ref, aged_ref):
    tokens, tiles, modes, members, per = dims
    for row in range(0, modes * tiles, HALF):
        state = get_rows(in_ref, per, row)
        for n in range(tokens // BLOCK):
            aged_ref[n, row : row + HALF, :] = state
            if n + 1 < tokens // BLOCK:
                state = state * end_ref[row : row + HALF, :]


def add_arrived(dims, aged_ref, taps_ref, y_ref, forward):
    tokens, tiles, modes, members, per = dims
    for h in range(0, tiles, HALF):
        rows = [i * tiles + h for i in range(modes)]

        def step(i, _):
            taps = [taps_ref[i + 1 if forward else i, row : row + HALF, :] for row in rows]
            for n in range(tokens // BLOCK):
                t = n * BLOCK + i
                at = tile(t if forward else tokens - 1 - t, tiles, h)
                parts = [x * aged_ref[n, row : row + HALF, :] for x, row in zip(taps, rows)]
                y_ref[at, :] = tree_sum(parts)
            return 0

        lax.fori_loop(0, BLOCK, step, 0, unroll=2)


def mix_kernel(
    dims, local_hbm, gate_hbm, cot_hbm, gain_hbm, a_ref, r_ref, in_ref, mixed_ref, sums_ref,
    local_ref, gate_ref, cot_ref, gain_ref, power_ref, taps_ref, aged_ref, y_ref, acc_ref, sem,
):
    tokens, tiles, modes, members, per = dims
    copies = fetch(
        [(local_hbm, local_ref), (gate_hbm, gate_ref), (cot_hbm, cot_ref), (gain_hbm, gain_ref)], sem
    )
    build_powers(r_ref, a_ref, taps_ref)
    block_power(a_ref, power_ref)
    age_states(dims, in_ref, power_ref, aged_ref)
    add_arrived(dims, aged_ref, taps_ref, y_ref, True)
    for copy in copies:
        copy.wait()

    def block(b, _):
        rows = pl.ds(pl.multiple_of(b * 16, 16), 16)
        squares = jnp.zeros((16, LANES), F32)
        inner = jnp.zeros((16, LANES), F32)
        for j in range(tiles):
            cols = slice(j * LANES, (j + 1) * LANES)
            at = pl.ds(b * 16 * tiles + j, 16, stride=tiles)
            mixed = y_ref[at, :] + local_ref[at, :]
            mixed_ref[rows, cols] = mixed
            premix = gate_ref[rows, cols].astype(F32) * mixed
            pull = cot_ref[rows, cols].astype(F32) * gain_ref[:, cols]
            squares = squares + premix * premix
            inner = inner + pull * premix
        acc_ref[0, rows, :] = squares
        acc_ref[1, rows, :] = inner
        return 0

    lax.fori_loop(0, tokens // 16, block, 0)
    for s in range(2):
        sums_ref[s : s + 1, :] = jnp.sum(acc_ref[s].T, axis=0, keepdims=True)


def norm_kernel(
    dims, width, sums_ref, mixed_ref, gate_ref, cot_ref, gain_ref, a_ref, in_ref, u_hbm, start_hbm, moment_hbm,
    w_ref, send_hbm, row_hbm, row_ref, send_ref, u_ref, start_ref, moment_ref, power_ref, aged_ref, part_ref, sem, out_sem,
):
    tokens, tiles, modes, members, per = dims
    copies = fetch([(u_hbm, u_ref), (start_hbm, start_ref), (moment_hbm, moment_ref)], sem)
    total = jnp.sum(sums_ref[...], axis=0)
    inverse = lax.rsqrt(total[0:1] / width + EPSILON)
    inner = inverse * total[1:2] / width
    row_ref[0] = jnp.broadcast_to(inverse, (LANES, tokens)).T
    row_ref[1] = jnp.broadcast_to(inner, (LANES, tokens)).T
    save = fetch([(row_ref, row_hbm)], out_sem, 2)

    def block(b, _):
        rows = pl.ds(pl.multiple_of(b * 16, 16), 16)
        inverse, inner = row_ref[0, rows, :], row_ref[1, rows, :]
        for j in range(tiles):
            cols = slice(j * LANES, (j + 1) * LANES)
            gate = gate_ref[rows, cols].astype(F32)
            normed = gate * mixed_ref[rows, cols] * inverse
            pull = cot_ref[rows, cols].astype(F32) * gain_ref[:, cols]
            dpre = (pull - normed * inner) * inverse
            w_ref[pl.ds(b * 16 * tiles + j, 16, stride=tiles), :] = dpre * gate
        return 0

    lax.fori_loop(0, tokens // 16, block, 0)

    build_powers(None, a_ref, power_ref)
    age_states(dims, in_ref, power_ref.at[BLOCK], aged_ref)
    copies[0].wait()

    blocks = tokens // BLOCK
    zero = jnp.zeros((HALF, LANES), F32)
    for h in range(0, tiles, HALF):

        def pairs(n, lags):
            lags = list(lags)
            us = []
            for i in range(BLOCK):
                at = tile(n * BLOCK + i, tiles, h)
                us.append(u_ref[at, :])
                w = w_ref[at, :]
                for lag in range(i + 1):
                    lags[lag] = lags[lag] + w * us[i - lag]
            return tuple(lags)

        lags = lax.fori_loop(0, blocks, pairs, (zero,) * BLOCK)
        scaled = [lag * float(i) for i, lag in enumerate(lags)]
        for r in range(modes):
            row = r * tiles + h
            decay = power_ref[1, row : row + HALF, :]
            first, second = lags[-1], scaled[-1]
            for i in range(BLOCK - 2, -1, -1):
                first = first * decay + lags[i]
                second = second * decay + scaled[i] if i else second * decay
            part_ref[0, row : row + HALF, :] = first
            part_ref[1, row : row + HALF, :] = second

    copies[1].wait()
    copies[2].wait()

    span = modes // 2
    out = []
    for first in range(0, modes, span):
        for h in range(0, tiles, HALF):
            rows = [(first + i) * tiles + h for i in range(span)]

            def step(m, carry):
                lead, res, mom = carry
                n = blocks - 1 - m
                xs = mx = None
                for i in range(BLOCK - 1, -1, -1):
                    w = w_ref[tile(n * BLOCK + i, tiles, h), :]
                    now = [power_ref[i + 1, row : row + HALF, :] * w for row in rows]
                    xs = now if xs is None else [x + y for x, y in zip(xs, now)]
                    mx = xs if mx is None else [x + y for x, y in zip(mx, xs)]
                aged = [aged_ref[n, row : row + HALF, :] for row in rows]
                states = [start_ref[n, row : row + HALF, :] + g for row, g in zip(rows, aged)]
                age = (n * BLOCK).astype(F32)
                moments = [moment_ref[n, row : row + HALF, :] + age * g for row, g in zip(rows, aged)]
                lead = [power_ref[BLOCK, row : row + HALF, :] * y + x for row, y, x in zip(rows, lead, xs)]
                res = [p + x * s for p, x, s in zip(res, xs, states)]
                mom = [p + y * s + x * t for p, y, s, x, t in zip(mom, mx, states, xs, moments)]
                return tuple(lead), tuple(res), tuple(mom)

            start = (
                (zero,) * span,
                tuple(part_ref[0, row : row + HALF, :] for row in rows),
                tuple(part_ref[1, row : row + HALF, :] for row in rows),
            )
            lead, res, mom = lax.fori_loop(0, blocks, step, start, unroll=2)
            for i, row in enumerate(rows):
                put_rows(send_ref, per, row, lead[i])
                for s, part in enumerate(member_sums(res[i], mom[i], members, per)):
                    last = (row // per + s) * (per + 1) + per
                    send_ref[last : last + 1, :] = part
        out += send_part(send_ref, send_hbm, out_sem, dims, first, span)
    for copy in save + out:
        copy.wait()


def back_kernel(
    dims, row_ref, mixed_ref, gate_ref, cot_ref, gain_ref, w_ref, a_ref, r_ref, skip_ref, out_ref, grad_q_ref, y_hbm,
    y_ref, sem,
):
    tokens, tiles, modes, members, per = dims

    def block(b, _):
        rows = pl.ds(pl.multiple_of(b * 16, 16), 16)
        inverse, inner = row_ref[0, rows, :], row_ref[1, rows, :]
        for j in range(tiles):
            cols = slice(j * LANES, (j + 1) * LANES)
            mixed = mixed_ref[rows, cols]
            gain = gain_ref[:, cols]
            normed = gate_ref[rows, cols].astype(F32) * mixed * inverse
            out_ref[rows, cols] = (normed * gain).astype(jnp.bfloat16)
            pull = cot_ref[rows, cols].astype(F32) * gain
            dpre = (pull - normed * inner) * inverse
            grad_q_ref[rows, cols] = (dpre * mixed).astype(jnp.bfloat16)
        return 0

    lax.fori_loop(0, tokens // 16, block, 0)
    zero = jnp.zeros((HALF, LANES), F32)
    for h in range(0, tiles, HALF):
        rows = [i * tiles + h for i in range(modes)]
        a = [a_ref[row : row + HALF, :] for row in rows]
        res = [r_ref[row : row + HALF, :] for row in rows]
        skip = skip_ref[h : h + HALF, :]

        def step(n, xs):
            for s in range(STEPS):
                at = tile(tokens - 1 - (n * STEPS + s), tiles, h)
                w = w_ref[at, :]
                bs = [x + w for x in xs]
                xs = [y * b for y, b in zip(a, bs)]
                y_ref[at, :] = tree_sum([x * z for x, z in zip(res, bs)]) + skip * w
            return tuple(xs)

        lax.fori_loop(0, tokens // STEPS, step, (zero,) * modes)
    for copy in fetch([(y_ref, y_hbm)], sem):
        copy.wait()


def suffix_kernel(dims, got_hbm, both_hbm, d_ref, after_hbm, send_ref, got_ref, both_ref, sem):
    tokens, tiles, modes, members, per = dims
    copies = fetch([(got_hbm, got_ref), (both_hbm, both_ref)], sem)
    for copy in copies:
        copy.wait()
    count = both_ref.shape[0]
    decay = d_ref[lax.axis_index("ctx")]
    after = mom = jnp.zeros((per, LANES), F32)
    part = jnp.zeros((1, LANES), F32)
    for i in range(count - 1, -1, -1):
        row = i * (per + 1)
        lead, both = got_ref[row : row + per, :], both_ref[i]
        before, moment = both[:per], both[per:]
        send_ref[row : row + per, :] = after
        aged = decay * after
        part = part + got_ref[row + per : row + per + 1, :]
        mom = mom + lead * moment + float(tokens) * aged * before
        after = aged + lead
    pad = max(HALF - per, 0)
    if pad:
        mom = jnp.concatenate([mom, jnp.zeros((pad, LANES), F32)], axis=0)
    part = part + member_sums(jnp.zeros_like(mom), mom, members, per)[0]
    for i in range(count):
        row = i * (per + 1) + per
        send_ref[row : row + 1, :] = part


def grad_kernel(
    dims, total_tokens, got_ref, local_hbm, k_hbm, v_hbm, a_ref, r_ref, residue_hbm, log_hbm,
    grad_k_ref, grad_v_ref, grad_res_ref, grad_log_ref,
    local_ref, k_ref, v_ref, residue_ref, log_ref, power_ref, taps_ref, aged_ref, y_ref, sem,
):
    tokens, tiles, modes, members, per = dims
    copies = fetch(
        [
            (local_hbm, local_ref), (k_hbm, k_ref), (v_hbm, v_ref),
            (residue_hbm, residue_ref), (log_hbm, log_ref),
        ],
        sem,
    )
    build_powers(r_ref, a_ref, taps_ref)
    block_power(a_ref, power_ref)
    age_states(dims, got_ref, power_ref, aged_ref)
    add_arrived(dims, aged_ref, taps_ref, y_ref, False)
    for copy in copies:
        copy.wait()

    def block(b, _):
        rows = pl.ds(pl.multiple_of(b * 16, 16), 16)
        for j in range(tiles):
            cols = slice(j * LANES, (j + 1) * LANES)
            at = pl.ds(b * 16 * tiles + j, 16, stride=tiles)
            grad = y_ref[at, :] + local_ref[at, :]
            grad_k_ref[rows, cols] = (grad * v_ref[rows, cols].astype(F32)).astype(jnp.bfloat16)
            grad_v_ref[rows, cols] = (grad * k_ref[rows, cols].astype(F32)).astype(jnp.bfloat16)
        return 0

    lax.fori_loop(0, tokens // 16, block, 0)

    groups = LANES // members
    lane = iota((modes, LANES), 1)
    first = second = jnp.zeros((modes, LANES), F32)
    for j in range(tiles):
        size = per + 1
        value = got_ref[pl.ds(j // per * size + per, modes, stride=tiles // per * size), :]
        at = 2 * groups * (j % per) + lane % groups
        own = lane // groups == j
        first = jnp.where(own, jnp.take_along_axis(value, at, axis=1), first)
        second = jnp.where(own, jnp.take_along_axis(value, groups + at, axis=1), second)
    grad_res_ref[...] = first / total_tokens
    grad_log_ref[...] = -residue_ref[...] * jnp.exp(log_ref[...]) * second / total_tokens


def call(kernel, name, outs, scratch=(), hbm=(), out_hbm=()):
    vmem, far = pl.BlockSpec(memory_space=pltpu.VMEM), pl.BlockSpec(memory_space=pltpu.HBM)

    def place(i, value):
        return pltpu.with_memory_space_constraint(value, pltpu.HBM) if i in hbm else value

    return lambda *args: pl.pallas_call(
        kernel,
        name=name,
        out_shape=[pltpu.HBM(s, d) if i in out_hbm else jax.ShapeDtypeStruct(s, d) for i, (s, d) in enumerate(outs)],
        in_specs=[far if i in hbm else vmem for i in range(len(args))],
        out_specs=[far if i in out_hbm else vmem for i in range(len(outs))],
        scratch_shapes=[pltpu.VMEM(*s) if isinstance(s, tuple) else s for s in scratch],
        compiler_params=pltpu.CompilerParams(vmem_limit_bytes=16 * 2**20),
    )(*(place(i, x) for i, x in enumerate(args)))


def per_device(out_gate, key_proj, value_proj, residue, log_decay, skip, gain, cotangent):
    tokens, channels = out_gate.shape
    groups, modes = residue.shape
    members, tiles = channels // groups, channels // LANES
    shards = lax.axis_size("ctx")
    width = float(channels * lax.axis_size("tp"))
    states = modes * tiles
    blocks = tokens // BLOCK
    per = states // shards
    dims = (tokens, tiles, modes, members, per)
    bf16 = jnp.bfloat16
    flat, state = ((tokens * tiles, LANES), F32), ((states, LANES), F32)
    powers, starts = ((BLOCK + 1, states, LANES), F32), ((blocks, states, LANES), F32)
    one, two = ((shards, per, LANES), F32), ((shards, 2 * per, LANES), F32)
    wide = ((shards * (per + 1), LANES), F32)
    narrow, small = ((tokens, channels), bf16), ((modes, groups), F32)
    rows = ((2, tokens, LANES), F32)
    line = ((1, channels), F32)
    skip, gain = skip.reshape(tiles, LANES), gain[None]
    residue, log_decay = residue.T, log_decay.T

    def exchange(value):
        shape = value.shape
        if len(shape) == 2:
            value = value.reshape(shards, 1, -1)
        return lax.all_to_all(value, "ctx", 0, 0, tiled=True).reshape(shape)

    def sems(n):
        return pltpu.SemaphoreType.DMA((n,))

    u, a, d, send = call(
        functools.partial(state_kernel, dims),
        "state",
        [flat, state, one, two],
        [narrow, narrow, small, state, powers, two, sems(9), sems(2)],
        hbm=(0, 1, 2),
        out_hbm=(3,),
    )(key_proj, value_proj, log_decay)
    got = exchange(send)
    r, far_u, local, start, moment = call(
        functools.partial(local_kernel, dims),
        "local",
        [state, flat, flat, starts, starts],
        [flat, starts, starts, sems(4)],
        out_hbm=(1, 2, 3, 4),
    )(u, a, residue, skip)
    both, send = call(functools.partial(prefix_kernel, per), "prefix", [two, one], hbm=(2,))(got, d, start)
    before = exchange(send)
    mixed, sums = call(
        functools.partial(mix_kernel, dims),
        "mix",
        [((tokens, channels), F32), ((2, tokens), F32)],
        [flat, narrow, narrow, line, state, powers, starts, flat, rows, sems(4)],
        hbm=(0, 1, 2, 3),
    )(local, out_gate, cotangent, gain, a, r, before)
    sums = lax.all_gather(sums, "tp")
    w, send, row = call(
        functools.partial(norm_kernel, dims, width),
        "norm",
        [flat, wide, rows],
        [rows, wide, flat, starts, starts, powers, starts, ((2, states, LANES), F32), sems(3), sems(3)],
        hbm=(7, 8, 9),
        out_hbm=(1, 2),
    )(sums, mixed, out_gate, cotangent, gain, a, before, far_u, start, moment)
    got = exchange(send)
    mixer_out, grad_q, local = call(functools.partial(back_kernel, dims), "back", [narrow, narrow, flat], [flat, sems(1)], out_hbm=(2,))(
        row, mixed, out_gate, cotangent, gain, w, a, r, skip
    )
    (send,) = call(functools.partial(suffix_kernel, dims), "suffix", [wide], [wide, two, sems(2)], hbm=(0, 1, 3))(got, both, d, grad_q)
    grad_k, grad_v, grad_residue, grad_log_decay = call(
        functools.partial(grad_kernel, dims, float(tokens * shards)),
        "grad",
        [narrow, narrow, small, small],
        [flat, narrow, narrow, small, small, state, powers, starts, flat, sems(5)],
        hbm=(1, 2, 3, 6, 7),
    )(exchange(send), local, key_proj, value_proj, a, r, residue, log_decay)
    return (mixer_out, grad_q, grad_k, grad_v, grad_residue.T, grad_log_decay.T)


def solution(mesh):
    tokens, split = P("ctx", "tp"), P("tp", None)
    return jax.shard_map(
        per_device,
        mesh=mesh,
        in_specs=(tokens, tokens, tokens, split, split, P("tp"), P("tp"), tokens),
        out_specs=(tokens, tokens, tokens, tokens, split, split),
        check_vma=False,
    )
```

```python
import functools

import jax
import jax.numpy as jnp
from jax import lax
from jax.experimental import pallas as pl
from jax.experimental.pallas import tpu as pltpu
from jax.sharding import PartitionSpec as P

EPSILON = 1e-06
F32 = jnp.float32
LANES = 128
HALF = 8
STEPS = 8
BLOCK = 16


def iota(shape, dim):
    return lax.broadcasted_iota(jnp.int32, shape, dim)


def get_rows(ref, per, row, base=0):
    pieces = range(row // per, (row + HALF) // per)
    if len(ref.shape) == 2:
        parts = [ref[p * (per + 1) : p * (per + 1) + per, :] for p in pieces]
    else:
        parts = [ref[p, base : base + per, :] for p in pieces]
    return jnp.concatenate(parts, axis=0)


def put_rows(ref, per, row, block, base=0):
    for s in range(HALF // per):
        p, part = row // per + s, block[s * per : (s + 1) * per]
        if len(ref.shape) == 2:
            ref[p * (per + 1) : p * (per + 1) + per, :] = part
        else:
            ref[p, base : base + per, :] = part


def member_sums(first, second, members, per):
    groups = LANES // members
    shift = 1
    while shift < members:
        first = first + pltpu.roll(first, LANES - shift, 1)
        second = second + pltpu.roll(second, LANES - shift, 1)
        shift *= 2
    row, lane = iota(first.shape, 0), iota(first.shape, 1)
    at = (lane % groups) * members
    first = jnp.take_along_axis(first, at, axis=1)
    second = jnp.take_along_axis(second, at, axis=1)
    value = jnp.where((lane // groups) % 2 == 0, first, second)
    value = jnp.where(lane // (2 * groups) == row % per, value, 0.0)
    return [jnp.sum(value[i : i + per], axis=0, keepdims=True) for i in range(0, first.shape[0], per)]


def expand(ref, out, tiles, members):
    modes = ref.shape[0]
    value = ref[...]
    lane = iota(value.shape, 1)
    for j in range(tiles):
        at = (LANES // members) * j + lane // members
        out[pl.ds(j, modes, stride=tiles), :] = jnp.take_along_axis(value, at, axis=1)


def tree_sum(parts):
    while len(parts) > 1:
        parts = [sum(parts[i : i + 2]) for i in range(0, len(parts), 2)]
    return parts[0]


def tile(t, tiles, h):
    return pl.ds(pl.multiple_of(t * tiles + h, HALF), HALF)


def build_powers(first, factor_ref, out_ref):
    for row in range(0, factor_ref.shape[0], HALF):
        factor = factor_ref[row : row + HALF, :]
        value = jnp.ones_like(factor) if first is None else first[row : row + HALF, :]
        for i in range(BLOCK + 1):
            out_ref[i, row : row + HALF, :] = value
            if i < BLOCK:
                value = value * factor


def block_power(a_ref, out_ref):
    for row in range(0, a_ref.shape[0], HALF):
        value, n = a_ref[row : row + HALF, :], 1
        while n < BLOCK:
            value, n = value * value, 2 * n
        out_ref[row : row + HALF, :] = value


def fetch(pairs, sem, base=0):
    copies = [pltpu.make_async_copy(a, b, sem.at[base + i]) for i, (a, b) in enumerate(pairs)]
    for copy in copies:
        copy.start()
    return copies


def send_part(send_ref, send_hbm, sem, dims, first, span):
    tokens, tiles, modes, members, per = dims
    size = per + 1 if len(send_ref.shape) == 2 else 1
    pieces = pl.ds(first * tiles // per * size, span * tiles // per * size)
    return fetch([(send_ref.at[pieces], send_hbm.at[pieces])], sem, first // span)


def state_kernel(
    dims, k_hbm, v_hbm, log_hbm, u_ref, a_ref, d_ref, send_hbm,
    k_ref, v_ref, log_ref, tab, power_ref, send_ref, sem, out_sem,
):
    tokens, tiles, modes, members, per = dims
    chunks = 4
    size = tokens // chunks
    (pull,) = fetch([(log_hbm, log_ref)], sem)
    copies = []
    for c in range(chunks):
        rows = pl.ds(c * size, size)
        pairs = [(k_hbm.at[rows, :], k_ref.at[rows, :]), (v_hbm.at[rows, :], v_ref.at[rows, :])]
        copies.append(fetch(pairs, sem, 1 + 2 * c))
    pull.wait()
    expand(log_ref, tab, tiles, members)
    for row in range(0, modes * tiles, HALF):
        rate = jnp.exp(tab[row : row + HALF, :])
        a_ref[row : row + HALF, :] = jnp.exp(-rate)
        put_rows(d_ref, per, row, jnp.exp(-rate * float(tokens)))
    build_powers(None, a_ref, power_ref)

    def fill(b, _):
        rows = pl.ds(pl.multiple_of(b * 16, 16), 16)
        for j in range(tiles):
            cols = slice(j * LANES, (j + 1) * LANES)
            u = k_ref[rows, cols].astype(F32) * v_ref[rows, cols].astype(F32)
            u_ref[pl.ds(b * 16 * tiles + j, 16, stride=tiles), :] = u
        return 0

    for c, pair in enumerate(copies):
        for copy in pair:
            copy.wait()
        lax.fori_loop(c * size // 16, (c + 1) * size // 16, fill, 0)

    span = modes // 2
    zero = jnp.zeros((HALF, LANES), F32)
    out = []
    for first in range(0, modes, span):
        for h in range(0, tiles, HALF):
            rows = [(first + i) * tiles + h for i in range(span)]

            def step(n, carry):
                hs, ms = carry
                xs = mx = None
                for i in range(BLOCK):
                    u = u_ref[tile(n * BLOCK + i, tiles, h), :]
                    if i == BLOCK - 1:
                        xs = [x + u for x in xs]
                        break
                    now = [power_ref[BLOCK - 1 - i, row : row + HALF, :] * u for row in rows]
                    xs = now if xs is None else [x + y for x, y in zip(xs, now)]
                    mx = xs if mx is None else [m + x for m, x in zip(mx, xs)]
                ends = [power_ref[BLOCK, row : row + HALF, :] for row in rows]
                ms = [e * (m + BLOCK * y) + x for e, m, y, x in zip(ends, ms, hs, mx)]
                hs = [e * y + x for e, y, x in zip(ends, hs, xs)]
                return tuple(hs), tuple(ms)

            hs, ms = lax.fori_loop(0, tokens // BLOCK, step, ((zero,) * span, (zero,) * span))
            for i, row in enumerate(rows):
                put_rows(send_ref, per, row, hs[i])
                put_rows(send_ref, per, row, ms[i], base=per)
        out += send_part(send_ref, send_hbm, out_sem, dims, first, span)
    for copy in out:
        copy.wait()


def local_kernel(
    dims, u_ref, a_ref, res_ref, skip_ref, r_ref, u_hbm, y_hbm, start_hbm, moment_hbm, y_ref, start_ref, moment_ref, sem
):
    tokens, tiles, modes, members, per = dims
    copies = fetch([(u_ref, u_hbm)], sem)
    expand(res_ref, r_ref, tiles, members)
    span = modes // 2
    zero = jnp.zeros((HALF, LANES), F32)
    for h in range(0, tiles, HALF):
        for first in range(0, modes, span):
            rows = [(first + i) * tiles + h for i in range(span)]
            a = [a_ref[row : row + HALF, :] for row in rows]
            res = [r_ref[row : row + HALF, :] for row in rows]
            skip = skip_ref[h : h + HALF, :]

            def step(n, carry):
                hs, ms = carry
                for i, row in enumerate(rows):
                    start_ref[n, row : row + HALF, :] = hs[i]
                    moment_ref[n, row : row + HALF, :] = ms[i]
                for s in range(BLOCK):
                    at = tile(n * BLOCK + s, tiles, h)
                    u = u_ref[at, :]
                    aged = [x * y for x, y in zip(a, hs)]
                    ms = [x * m + y for x, m, y in zip(a, ms, aged)]
                    hs = [y + u for y in aged]
                    y = tree_sum([x * z for x, z in zip(res, hs)])
                    y_ref[at, :] = (y_ref[at, :] if first else skip * u) + y
                return tuple(hs), tuple(ms)

            lax.fori_loop(0, tokens // BLOCK, step, ((zero,) * span, (zero,) * span))
    copies += fetch([(y_ref, y_hbm), (start_ref, start_hbm), (moment_ref, moment_hbm)], sem, 1)
    for copy in copies:
        copy.wait()


def prefix_kernel(per, got_ref, d_ref, after_hbm, both_ref, send_ref):
    count = got_ref.shape[0]
    decay = d_ref[lax.axis_index("ctx")]
    decay = jnp.concatenate([decay, decay], axis=0)

    def step(i, before):
        both_ref[i] = before
        send_ref[i] = before[:per]
        return decay * before + got_ref[i]

    lax.fori_loop(0, count, step, jnp.zeros(decay.shape, F32), unroll=8)


def age_states(dims, in_ref, end_ref, aged_ref):
    tokens, tiles, modes, members, per = dims
    for row in range(0, modes * tiles, HALF):
        state = get_rows(in_ref, per, row)
        for n in range(tokens // BLOCK):
            aged_ref[n, row : row + HALF, :] = state
            if n + 1 < tokens // BLOCK:
                state = state * end_ref[row : row + HALF, :]


def add_arrived(dims, aged_ref, taps_ref, y_ref, forward):
    tokens, tiles, modes, members, per = dims
    for h in range(0, tiles, HALF):
        rows = [i * tiles + h for i in range(modes)]

        def step(i, _):
            taps = [taps_ref[i + 1 if forward else i, row : row + HALF, :] for row in rows]
            for n in range(tokens // BLOCK):
                t = n * BLOCK + i
                at = tile(t if forward else tokens - 1 - t, tiles, h)
                parts = [x * aged_ref[n, row : row + HALF, :] for x, row in zip(taps, rows)]
                y_ref[at, :] = tree_sum(parts)
            return 0

        lax.fori_loop(0, BLOCK, step, 0, unroll=2)


def mix_kernel(
    dims, local_hbm, gate_hbm, cot_hbm, gain_hbm, a_ref, r_ref, in_ref, mixed_ref, sums_ref,
    local_ref, gate_ref, cot_ref, gain_ref, power_ref, taps_ref, aged_ref, y_ref, acc_ref, sem,
):
    tokens, tiles, modes, members, per = dims
    copies = fetch(
        [(local_hbm, local_ref), (gate_hbm, gate_ref), (cot_hbm, cot_ref), (gain_hbm, gain_ref)], sem
    )
    build_powers(r_ref, a_ref, taps_ref)
    block_power(a_ref, power_ref)
    age_states(dims, in_ref, power_ref, aged_ref)
    add_arrived(dims, aged_ref, taps_ref, y_ref, True)
    for copy in copies:
        copy.wait()

    def block(b, _):
        rows = pl.ds(pl.multiple_of(b * 16, 16), 16)
        squares = jnp.zeros((16, LANES), F32)
        inner = jnp.zeros((16, LANES), F32)
        for j in range(tiles):
            cols = slice(j * LANES, (j + 1) * LANES)
            at = pl.ds(b * 16 * tiles + j, 16, stride=tiles)
            mixed = y_ref[at, :] + local_ref[at, :]
            mixed_ref[rows, cols] = mixed
            premix = gate_ref[rows, cols].astype(F32) * mixed
            pull = cot_ref[rows, cols].astype(F32) * gain_ref[:, cols]
            squares = squares + premix * premix
            inner = inner + pull * premix
        acc_ref[0, rows, :] = squares
        acc_ref[1, rows, :] = inner
        return 0

    lax.fori_loop(0, tokens // 16, block, 0)
    for s in range(2):
        sums_ref[s : s + 1, :] = jnp.sum(acc_ref[s].T, axis=0, keepdims=True)


def norm_kernel(
    dims, width, sums_ref, mixed_ref, gate_ref, cot_ref, gain_ref, a_ref, in_ref, u_hbm, start_hbm, moment_hbm,
    w_ref, send_hbm, row_hbm, row_ref, send_ref, u_ref, start_ref, moment_ref, power_ref, aged_ref, part_ref, sem, out_sem,
):
    tokens, tiles, modes, members, per = dims
    copies = fetch([(u_hbm, u_ref), (start_hbm, start_ref), (moment_hbm, moment_ref)], sem)
    total = jnp.sum(sums_ref[...], axis=0)
    inverse = lax.rsqrt(total[0:1] / width + EPSILON)
    inner = inverse * total[1:2] / width
    row_ref[0] = jnp.broadcast_to(inverse, (LANES, tokens)).T
    row_ref[1] = jnp.broadcast_to(inner, (LANES, tokens)).T
    save = fetch([(row_ref, row_hbm)], out_sem, 2)

    def block(b, _):
        rows = pl.ds(pl.multiple_of(b * 16, 16), 16)
        inverse, inner = row_ref[0, rows, :], row_ref[1, rows, :]
        for j in range(tiles):
            cols = slice(j * LANES, (j + 1) * LANES)
            gate = gate_ref[rows, cols].astype(F32)
            normed = gate * mixed_ref[rows, cols] * inverse
            pull = cot_ref[rows, cols].astype(F32) * gain_ref[:, cols]
            dpre = (pull - normed * inner) * inverse
            w_ref[pl.ds(b * 16 * tiles + j, 16, stride=tiles), :] = dpre * gate
        return 0

    lax.fori_loop(0, tokens // 16, block, 0)

    build_powers(None, a_ref, power_ref)
    age_states(dims, in_ref, power_ref.at[BLOCK], aged_ref)
    copies[0].wait()

    blocks = tokens // BLOCK
    zero = jnp.zeros((HALF, LANES), F32)
    for h in range(0, tiles, HALF):

        def pairs(n, lags):
            lags = list(lags)
            us = []
            for i in range(BLOCK):
                at = tile(n * BLOCK + i, tiles, h)
                us.append(u_ref[at, :])
                w = w_ref[at, :]
                for lag in range(i + 1):
                    lags[lag] = lags[lag] + w * us[i - lag]
            return tuple(lags)

        lags = lax.fori_loop(0, blocks, pairs, (zero,) * BLOCK)
        scaled = [lag * float(i) for i, lag in enumerate(lags)]
        for r in range(modes):
            row = r * tiles + h
            decay = power_ref[1, row : row + HALF, :]
            first, second = lags[-1], scaled[-1]
            for i in range(BLOCK - 2, -1, -1):
                first = first * decay + lags[i]
                second = second * decay + scaled[i] if i else second * decay
            part_ref[0, row : row + HALF, :] = first
            part_ref[1, row : row + HALF, :] = second

    copies[1].wait()
    copies[2].wait()

    span = modes // 2
    out = []
    for first in range(0, modes, span):
        for h in range(0, tiles, HALF):
            rows = [(first + i) * tiles + h for i in range(span)]

            def step(m, carry):
                lead, res, mom = carry
                n = blocks - 1 - m
                xs = mx = None
                for i in range(BLOCK - 1, -1, -1):
                    w = w_ref[tile(n * BLOCK + i, tiles, h), :]
                    now = [power_ref[i + 1, row : row + HALF, :] * w for row in rows]
                    xs = now if xs is None else [x + y for x, y in zip(xs, now)]
                    mx = xs if mx is None else [x + y for x, y in zip(mx, xs)]
                aged = [aged_ref[n, row : row + HALF, :] for row in rows]
                states = [start_ref[n, row : row + HALF, :] + g for row, g in zip(rows, aged)]
                age = (n * BLOCK).astype(F32)
                moments = [moment_ref[n, row : row + HALF, :] + age * g for row, g in zip(rows, aged)]
                lead = [power_ref[BLOCK, row : row + HALF, :] * y + x for row, y, x in zip(rows, lead, xs)]
                res = [p + x * s for p, x, s in zip(res, xs, states)]
                mom = [p + y * s + x * t for p, y, s, x, t in zip(mom, mx, states, xs, moments)]
                return tuple(lead), tuple(res), tuple(mom)

            start = (
                (zero,) * span,
                tuple(part_ref[0, row : row + HALF, :] for row in rows),
                tuple(part_ref[1, row : row + HALF, :] for row in rows),
            )
            lead, res, mom = lax.fori_loop(0, blocks, step, start, unroll=2)
            for i, row in enumerate(rows):
                put_rows(send_ref, per, row, lead[i])
                for s, part in enumerate(member_sums(res[i], mom[i], members, per)):
                    last = (row // per + s) * (per + 1) + per
                    send_ref[last : last + 1, :] = part
        out += send_part(send_ref, send_hbm, out_sem, dims, first, span)
    for copy in save + out:
        copy.wait()


def back_kernel(
    dims, row_hbm, mixed_ref, gate_hbm, cot_hbm, gain_ref, w_ref, a_ref, r_ref, skip_ref, both_hbm,
    out_ref, grad_q_ref, y_hbm, both_ref, row_ref, gate_ref, cot_ref, y_ref, sem,
):
    tokens, tiles, modes, members, per = dims
    pairs = [(row_hbm, row_ref), (gate_hbm, gate_ref), (cot_hbm, cot_ref), (both_hbm, both_ref)]
    for copy in fetch(pairs, sem, 1):
        copy.wait()

    def block(b, _):
        rows = pl.ds(pl.multiple_of(b * 16, 16), 16)
        inverse, inner = row_ref[0, rows, :], row_ref[1, rows, :]
        for j in range(tiles):
            cols = slice(j * LANES, (j + 1) * LANES)
            mixed = mixed_ref[rows, cols]
            gain = gain_ref[:, cols]
            normed = gate_ref[rows, cols].astype(F32) * mixed * inverse
            out_ref[rows, cols] = (normed * gain).astype(jnp.bfloat16)
            pull = cot_ref[rows, cols].astype(F32) * gain
            dpre = (pull - normed * inner) * inverse
            grad_q_ref[rows, cols] = (dpre * mixed).astype(jnp.bfloat16)
        return 0

    lax.fori_loop(0, tokens // 16, block, 0)
    zero = jnp.zeros((HALF, LANES), F32)
    for h in range(0, tiles, HALF):
        rows = [i * tiles + h for i in range(modes)]
        a = [a_ref[row : row + HALF, :] for row in rows]
        res = [r_ref[row : row + HALF, :] for row in rows]
        skip = skip_ref[h : h + HALF, :]

        def step(n, xs):
            for s in range(STEPS):
                at = tile(tokens - 1 - (n * STEPS + s), tiles, h)
                w = w_ref[at, :]
                bs = [x + w for x in xs]
                xs = [y * b for y, b in zip(a, bs)]
                y_ref[at, :] = tree_sum([x * z for x, z in zip(res, bs)]) + skip * w
            return tuple(xs)

        lax.fori_loop(0, tokens // STEPS, step, (zero,) * modes)
    for copy in fetch([(y_ref, y_hbm)], sem):
        copy.wait()


def suffix_kernel(dims, got_ref, both_ref, d_ref, send_ref):
    tokens, tiles, modes, members, per = dims
    count = both_ref.shape[0]
    decay = d_ref[lax.axis_index("ctx")]
    after = mom = jnp.zeros((per, LANES), F32)
    part = jnp.zeros((1, LANES), F32)
    for i in range(count - 1, -1, -1):
        row = i * (per + 1)
        lead, both = got_ref[row : row + per, :], both_ref[i]
        before, moment = both[:per], both[per:]
        send_ref[row : row + per, :] = after
        aged = decay * after
        part = part + got_ref[row + per : row + per + 1, :]
        mom = mom + lead * moment + float(tokens) * aged * before
        after = aged + lead
    pad = max(HALF - per, 0)
    if pad:
        mom = jnp.concatenate([mom, jnp.zeros((pad, LANES), F32)], axis=0)
    part = part + member_sums(jnp.zeros_like(mom), mom, members, per)[0]
    for i in range(count):
        row = i * (per + 1) + per
        send_ref[row : row + 1, :] = part


def grad_kernel(
    dims, total_tokens, got_ref, local_hbm, k_hbm, v_hbm, a_ref, r_ref, residue_hbm, log_hbm,
    grad_k_hbm, grad_v_hbm, grad_res_hbm, grad_log_hbm,
    grad_k_ref, grad_v_ref, grad_res_ref, grad_log_ref, local_ref, k_ref, v_ref, residue_ref, log_ref, power_ref, taps_ref, aged_ref, y_ref, sem, out_sem,
):
    tokens, tiles, modes, members, per = dims
    copies = fetch(
        [
            (local_hbm, local_ref), (k_hbm, k_ref), (v_hbm, v_ref),
            (residue_hbm, residue_ref), (log_hbm, log_ref),
        ],
        sem,
    )
    build_powers(r_ref, a_ref, taps_ref)
    block_power(a_ref, power_ref)
    age_states(dims, got_ref, power_ref, aged_ref)
    add_arrived(dims, aged_ref, taps_ref, y_ref, False)
    for copy in copies:
        copy.wait()
    groups = LANES // members
    lane = iota((modes, LANES), 1)
    first = second = jnp.zeros((modes, LANES), F32)
    for j in range(tiles):
        size = per + 1
        value = got_ref[pl.ds(j // per * size + per, modes, stride=tiles // per * size), :]
        at = 2 * groups * (j % per) + lane % groups
        own = lane // groups == j
        first = jnp.where(own, jnp.take_along_axis(value, at, axis=1), first)
        second = jnp.where(own, jnp.take_along_axis(value, groups + at, axis=1), second)
    grad_res_ref[...] = first / total_tokens
    grad_log_ref[...] = -residue_ref[...] * jnp.exp(log_ref[...]) * second / total_tokens
    copies = fetch([(grad_res_ref, grad_res_hbm), (grad_log_ref, grad_log_hbm)], out_sem)

    def halves(b):
        rows = pl.ds(pl.multiple_of(b * 16, 16), 16)
        return [
            pltpu.make_async_copy(grad_k_ref.at[rows, :], grad_k_hbm.at[rows, :], out_sem.at[2 + 2 * b]),
            pltpu.make_async_copy(grad_v_ref.at[rows, :], grad_v_hbm.at[rows, :], out_sem.at[3 + 2 * b]),
        ]

    def block(b, _):
        rows = pl.ds(pl.multiple_of(b * 16, 16), 16)
        for j in range(tiles):
            cols = slice(j * LANES, (j + 1) * LANES)
            at = pl.ds(b * 16 * tiles + j, 16, stride=tiles)
            grad = y_ref[at, :] + local_ref[at, :]
            grad_k_ref[rows, cols] = (grad * v_ref[rows, cols].astype(F32)).astype(jnp.bfloat16)
            grad_v_ref[rows, cols] = (grad * k_ref[rows, cols].astype(F32)).astype(jnp.bfloat16)
        for copy in halves(b):
            copy.start()
        return 0

    lax.fori_loop(0, tokens // 16, block, 0)
    for b in range(tokens // 16):
        copies += halves(b)
    for copy in copies:
        copy.wait()


def call(kernel, name, outs, scratch=(), hbm=(), out_hbm=()):
    vmem, far = pl.BlockSpec(memory_space=pltpu.VMEM), pl.BlockSpec(memory_space=pltpu.HBM)

    def place(i, value):
        return pltpu.with_memory_space_constraint(value, pltpu.HBM) if i in hbm else value

    return lambda *args: pl.pallas_call(
        kernel,
        name=name,
        out_shape=[pltpu.HBM(s, d) if i in out_hbm else jax.ShapeDtypeStruct(s, d) for i, (s, d) in enumerate(outs)],
        in_specs=[far if i in hbm else vmem for i in range(len(args))],
        out_specs=[far if i in out_hbm else vmem for i in range(len(outs))],
        scratch_shapes=[pltpu.VMEM(*s) if isinstance(s, tuple) else s for s in scratch],
        compiler_params=pltpu.CompilerParams(vmem_limit_bytes=16 * 2**20),
    )(*(place(i, x) for i, x in enumerate(args)))


def per_device(out_gate, key_proj, value_proj, residue, log_decay, skip, gain, cotangent):
    tokens, channels = out_gate.shape
    groups, modes = residue.shape
    members, tiles = channels // groups, channels // LANES
    shards = lax.axis_size("ctx")
    width = float(channels * lax.axis_size("tp"))
    states = modes * tiles
    blocks = tokens // BLOCK
    per = states // shards
    dims = (tokens, tiles, modes, members, per)
    bf16 = jnp.bfloat16
    flat, state = ((tokens * tiles, LANES), F32), ((states, LANES), F32)
    powers, starts = ((BLOCK + 1, states, LANES), F32), ((blocks, states, LANES), F32)
    one, two = ((shards, per, LANES), F32), ((shards, 2 * per, LANES), F32)
    wide = ((shards * (per + 1), LANES), F32)
    narrow, small = ((tokens, channels), bf16), ((modes, groups), F32)
    rows = ((2, tokens, LANES), F32)
    line = ((1, channels), F32)
    skip, gain = skip.reshape(tiles, LANES), gain[None]
    residue, log_decay = residue.T, log_decay.T

    def exchange(value):
        shape = value.shape
        if len(shape) == 2:
            value = value.reshape(shards, 1, -1)
        return lax.all_to_all(value, "ctx", 0, 0, tiled=True).reshape(shape)

    def sems(n):
        return pltpu.SemaphoreType.DMA((n,))

    u, a, d, send = call(
        functools.partial(state_kernel, dims),
        "state",
        [flat, state, one, two],
        [narrow, narrow, small, state, powers, two, sems(9), sems(2)],
        hbm=(0, 1, 2),
        out_hbm=(3,),
    )(key_proj, value_proj, log_decay)
    got = exchange(send)
    r, far_u, local, start, moment = call(
        functools.partial(local_kernel, dims),
        "local",
        [state, flat, flat, starts, starts],
        [flat, starts, starts, sems(4)],
        out_hbm=(1, 2, 3, 4),
    )(u, a, residue, skip)
    both, send = call(functools.partial(prefix_kernel, per), "prefix", [two, one], hbm=(2,))(got, d, start)
    before = exchange(send)
    mixed, sums = call(
        functools.partial(mix_kernel, dims),
        "mix",
        [((tokens, channels), F32), ((2, tokens), F32)],
        [flat, narrow, narrow, line, state, powers, starts, flat, rows, sems(4)],
        hbm=(0, 1, 2, 3),
    )(local, out_gate, cotangent, gain, a, r, before)
    sums = lax.all_gather(sums, "tp")
    w, send, row = call(
        functools.partial(norm_kernel, dims, width),
        "norm",
        [flat, wide, rows],
        [rows, wide, flat, starts, starts, powers, starts, ((2, states, LANES), F32), sems(3), sems(3)],
        hbm=(7, 8, 9),
        out_hbm=(1, 2),
    )(sums, mixed, out_gate, cotangent, gain, a, before, far_u, start, moment)
    got = exchange(send)
    mixer_out, grad_q, local, both = call(
        functools.partial(back_kernel, dims),
        "back",
        [narrow, narrow, flat, two],
        [rows, narrow, narrow, flat, sems(5)],
        hbm=(0, 2, 3, 9),
        out_hbm=(2,),
    )(row, mixed, out_gate, cotangent, gain, w, a, r, skip, both)
    (send,) = call(functools.partial(suffix_kernel, dims), "suffix", [wide])(got, both, d)
    grad_k, grad_v, grad_residue, grad_log_decay = call(
        functools.partial(grad_kernel, dims, float(tokens * shards)),
        "grad",
        [narrow, narrow, small, small],
        [narrow, narrow, small, small, flat, narrow, narrow, small, small, state, powers, starts, flat, sems(5), sems(2 + tokens // 8)],
        hbm=(1, 2, 3, 6, 7),
        out_hbm=(0, 1, 2, 3),
    )(exchange(send), local, key_proj, value_proj, a, r, residue, log_decay)
    return (mixer_out, grad_q, grad_k, grad_v, grad_residue.T, grad_log_decay.T)


def solution(mesh):
    tokens, split = P("ctx", "tp"), P("tp", None)
    return jax.shard_map(
        per_device,
        mesh=mesh,
        in_specs=(tokens, tokens, tokens, split, split, P("tp"), P("tp"), tokens),
        out_specs=(tokens, tokens, tokens, tokens, split, split),
        check_vma=False,
    )
```
